32 devices in a mesh: doc: 8 (over z, core), seq: 4 (over y, x).
Axes of the slice: x: 2, y: 2, z: 4, core: 2. Of those that a mesh axis runs over, the one named last changes fastest.
Arguments:
- tokens: bfloat16 [8, 1536, 2048], P('doc', 'seq'), may hold values from -6 to 6
- norm_gain: float32 [2048], replicated, may hold values from 0.5 to 1.5
- in_weight: bfloat16 [2048, 4096], P('doc'), may hold values from -0.125 to 0.125
- conv_weight: float32 [4, 4096], replicated, may hold values from -3 to 3
- conv_bias: float32 [4096], replicated, may hold values from -3 to 3
- state_weight: bfloat16 [4096, 32], replicated, may hold values from -0.01171875 to 0.01171875
- skip_gain: float32 [4096], replicated, may hold values from 0.1 to 1.9
- retention: float32 [8, 1536, 64], P('doc', 'seq'), may hold values from 0.6 to 1
Outputs:
- scanned: bfloat16 [8, 1536, 4096], P('doc', 'seq')
The draws below stay inside these ranges and needn't reach their ends.
All inputs are finite; a program needn't handle non-finite values.
Results may differ from the reference program's by a relative error of at most 0.007.
Values may be sent and summed in bfloat16 or wider, within the bound.
A program may use at most 128 MiB of HBM per device.

```python
import math
import jax
import jax.numpy as jnp
from jax import lax

D = 2048
DI = 4096
STATE = 16
HEAD = 64
KERNEL = 4
L_DEV = 384
RETENTION_HEADS = 64
SEQUENCE_LENGTH = 1536
DOCUMENT_COUNT = 8


def draw_retention(key, part):
    parallel_lanes = jax.random.split(key, 7)
    slow_share = 0.5
    slow_heads = jax.random.uniform(parallel_lanes[0], (DOCUMENT_COUNT, 1, RETENTION_HEADS)) < slow_share
    slow_rate = jnp.exp(jax.random.uniform(parallel_lanes[1], (DOCUMENT_COUNT, 1, RETENTION_HEADS), minval=math.log(0.03), maxval=math.log(0.3))) / SEQUENCE_LENGTH
    fast_rate = jax.random.uniform(parallel_lanes[2], (DOCUMENT_COUNT, 1, RETENTION_HEADS), minval=1.0 / 40.0, maxval=1.0 / 25.0)
    base_rate = jnp.where(slow_heads, slow_rate, fast_rate)
    token_factor = jnp.exp(jax.random.uniform(parallel_lanes[3], (DOCUMENT_COUNT, SEQUENCE_LENGTH, RETENTION_HEADS), minval=math.log(0.7), maxval=math.log(1.4)))
    shard_factor = jnp.exp(jax.random.uniform(parallel_lanes[4], (DOCUMENT_COUNT, SEQUENCE_LENGTH // L_DEV, 1, RETENTION_HEADS), minval=math.log(0.5), maxval=math.log(2.0)))
    shard_factor = jnp.broadcast_to(shard_factor, (DOCUMENT_COUNT, SEQUENCE_LENGTH // L_DEV, L_DEV, RETENTION_HEADS)).reshape(DOCUMENT_COUNT, SEQUENCE_LENGTH, RETENTION_HEADS)
    retained_state = jnp.exp(-base_rate * token_factor * shard_factor)
    spike_places = jax.random.randint(parallel_lanes[5], (DOCUMENT_COUNT, 2), 0, SEQUENCE_LENGTH)
    token_places = jnp.arange(SEQUENCE_LENGTH, dtype=jnp.int32)
    spiking_mask = jnp.any(token_places[None, :, None] == spike_places[:, None, :], axis=-1)
    spike_value = jax.random.uniform(parallel_lanes[6], (DOCUMENT_COUNT, SEQUENCE_LENGTH, RETENTION_HEADS), minval=0.6, maxval=0.8)
    return jnp.where(spiking_mask[:, :, None], spike_value, retained_state).astype(jnp.float32)


def shard_levels(key, dims, cuts, low, high):
    factor_of, own = 1.0, jax.random.fold_in(key, 6)
    for dim, blocks in cuts:
        steps = jnp.exp(jax.random.uniform(jax.random.fold_in(own, dim), (blocks,), jnp.float32, low / len(cuts), high / len(cuts)))
        factor_of = factor_of * jnp.repeat(steps, dims[dim] // blocks).reshape([-1 if axis == dim else 1 for axis in range(len(dims))])
    return factor_of


def noise(rng, dims, deviation, limit, shards=(), kind=jnp.bfloat16):
    level = shard_levels(rng, dims, shards, -0.22, 0.18) if shards else 1.0
    values = jax.random.normal(rng, dims, jnp.float32) * deviation * level
    return jnp.minimum(jnp.maximum(values, -limit), limit).astype(kind)


def setup_inputs(seed: int = 0) -> dict:
    key_list = jax.random.split(jax.random.key(seed), 9)
    tokens = noise(key_list[0], (DOCUMENT_COUNT, SEQUENCE_LENGTH, D), 1.0, 6.0, ((0, 8), (1, 4)))
    norm_gain = jnp.clip(1.0 + 0.1 * jax.random.normal(key_list[1], (D,), jnp.float32), 0.5, 1.5)
    in_weight = noise(key_list[2], (D, DI), D ** -0.5, 0.125, ((0, 8),))
    conv_weight = noise(key_list[3], (KERNEL, DI), KERNEL ** -0.5, 3.0, (), jnp.float32)
    conv_bias = noise(key_list[4], (DI,), 0.5, 3.0, (), jnp.float32)
    state_weight = noise(key_list[5], (DI, 2 * STATE), (DI * 64) ** -0.5, 0.01171875)
    skip_gain = jnp.clip(1.0 + 0.18 * jax.random.normal(key_list[6], (DI,), jnp.float32), 0.1, 1.9)
    retention = draw_retention(jax.random.fold_in(key_list[8], 71), 0)
    return dict(tokens=tokens, norm_gain=norm_gain, in_weight=in_weight, conv_weight=conv_weight, conv_bias=conv_bias, state_weight=state_weight, skip_gain=skip_gain, retention=retention)


def rms_rows(row_block, gain_row):
    values = row_block.astype(jnp.float32)
    inverse_rms = lax.rsqrt(lax.optimization_barrier(jnp.mean(values * values, axis=-1, keepdims=True)) + 1e-05)
    return (values * inverse_rms * gain_row.astype(jnp.float32)).astype(jnp.bfloat16)

def reference(tokens, norm_gain, in_weight, conv_weight, conv_bias, state_weight, skip_gain, retention):

    def one_document(inputs):
        document, retained_state = inputs
        normed = rms_rows(document, norm_gain)
        projected = jnp.dot(normed, in_weight, preferred_element_type=jnp.float32).astype(jnp.bfloat16)
        padded = jnp.pad(projected.astype(jnp.float32), ((KERNEL - 1, 0), (0, 0)))
        convolved = jnp.zeros((SEQUENCE_LENGTH, DI), jnp.float32) + conv_bias.astype(jnp.float32)
        for offset in range(KERNEL):
            convolved = convolved + conv_weight[offset].astype(jnp.float32) * padded[offset:offset + SEQUENCE_LENGTH]
        activated = jax.nn.silu(convolved).astype(jnp.bfloat16)
        maps = jnp.dot(activated, state_weight, preferred_element_type=jnp.float32)
        input_map = maps[:, :STATE]
        output_map = maps[:, STATE:]
        channels = activated.astype(jnp.float32).reshape(SEQUENCE_LENGTH, RETENTION_HEADS, HEAD)

        def advance(hidden_state, position):
            kept_now, channel_now, input_now, output_now = position
            hidden_state = kept_now[:, None, None] * hidden_state + channel_now[:, :, None] * input_now[None, None, :]
            emitted = lax.optimization_barrier(jnp.sum(hidden_state * output_now[None, None, :], axis=-1))
            return (hidden_state, emitted)
        start_state = jnp.zeros((RETENTION_HEADS, HEAD, STATE), jnp.float32)
        _, emitted_all = lax.scan(advance, start_state, (retained_state, channels, input_map, output_map))
        result = emitted_all.reshape(SEQUENCE_LENGTH, DI) + skip_gain.astype(jnp.float32) * activated.astype(jnp.float32)
        return result.astype(jnp.bfloat16)
    return lax.map(one_document, (tokens, retention))
```

```python
import functools
import jax
import jax.numpy as jnp
from jax import lax
from jax.experimental import pallas as pl
from jax.experimental.pallas import tpu as pltpu
from jax.sharding import PartitionSpec as P

BLOCK = 128
LANES = 128
HALO = 16
WIDTH = 2048
SUBS = 2
COMMON = 8
LAG_PLANE = 3
LAG_DIAG = 6
LAG_COMMON = 4
MESH = pl.DeviceIdType.MESH
HBM = pl.BlockSpec(memory_space=pl.ANY)
ONCHIP = pl.BlockSpec(memory_space=pltpu.VMEM)


def gather_kernel(planes, shard, tokens, full, halo, local_sem, own_send, own_recv, halo_send,
                  halo_recv, line_send, line_recv, px_send, px_recv, py_send, py_recv, dx_send,
                  dx_recv, dy_send, dy_recv, com_send, com_recv,
                  sib_send, sib_recv, bounce):
    doc = lax.axis_index("doc")
    seq = lax.axis_index("seq")
    z = lax.div(doc, 2)
    core = lax.rem(doc, 2)
    depth, width = shard.shape
    common = width // COMMON
    quarter = (width - common) // 4
    rows = depth // SUBS
    tail = tokens.at[0, pl.ds(tokens.shape[1] - HALO, HALO)]
    xn = seq + 1 - 2 * lax.rem(seq, 2)
    yn = lax.rem(seq + 2, 4)
    dn = 3 - seq
    follower = lax.rem(seq + 1, 4)
    leader = lax.rem(seq + 3, 4)
    sibling = (doc + 1 - 2 * core, seq)

    barrier = pltpu.get_barrier_semaphore()
    for peer in (xn, yn, dn):
        pl.semaphore_signal(barrier, inc=1, device_id=(doc, peer), device_id_type=MESH)
    pl.semaphore_signal(barrier, inc=1, device_id=sibling, device_id_type=MESH)

    @pl.when(z > 0)
    def _():
        pl.semaphore_signal(barrier, inc=1, device_id=(doc - 2, seq), device_id_type=MESH)

    @pl.when(z < planes - 1)
    def _():
        pl.semaphore_signal(barrier, inc=1, device_id=(doc + 2, seq), device_id_type=MESH)

    ends = jnp.where(z > 0, 1, 0) + jnp.where(z < planes - 1, 1, 0)
    pl.semaphore_wait(barrier, 4 + ends)

    def piece(ref, owner, sub, column, start=0, count=rows):
        if column is None:
            columns = pl.ds(4 * quarter, common)
        else:
            columns = pl.ds(pl.multiple_of(column * quarter, LANES), quarter)
        if owner is None:
            return ref.at[pl.ds(sub * rows + start, count), columns]
        return ref.at[owner, pl.ds(sub * rows + start, count), columns]

    def remote(source, target, send, recv, device):
        return pltpu.make_async_remote_copy(
            src_ref=source, dst_ref=target, send_sem=send, recv_sem=recv,
            device_id=device, device_id_type=MESH)

    items = [(k, u, side) for k in range(1, planes) for u in range(SUBS) for side in range(2)]
    place = {item: i for i, item in enumerate(items)}

    def plane_of(item):
        return z - item[0] if item[2] == 0 else z + item[0]

    def exists(item):
        return plane_of(item) >= 0 if item[2] == 0 else plane_of(item) < planes

    def onward(item):
        there = z < planes - 1 if item[2] == 0 else z > 0
        return jnp.logical_and(exists(item), there) if item[0] > 0 else there

    def line_copy(item):
        i = place[(item[0] + 1, item[1], item[2])]
        owner = 2 * plane_of(item) + core
        target = piece(full, owner, item[1], seq)
        source = piece(shard, None, item[1], seq) if item[0] == 0 else target
        device = (doc + 2, seq) if item[2] == 0 else (doc - 2, seq)
        return remote(source, target, line_send.at[i], line_recv.at[i], device)

    def common_copy(item):
        i = place[(item[0] + 1, item[1], item[2])]
        owner = 2 * plane_of(item) + core
        target = piece(full, owner, item[1], None)
        source = piece(shard, None, item[1], None) if item[0] == 0 else target
        device = (doc + 2, seq) if item[2] == 0 else (doc - 2, seq)
        return remote(source, target, com_send.at[i], com_recv.at[i], device)

    def common_arrival(item):
        i = place[item]
        target = piece(full, 2 * plane_of(item) + core, item[1], None)
        return remote(target, target, com_send.at[i], com_recv.at[i], sibling)

    def line_arrival(item):
        i = place[item]
        target = piece(full, 2 * plane_of(item) + core, item[1], seq)
        return remote(target, target, line_send.at[i], line_recv.at[i], sibling)

    def plane_copies(item, mine):
        i = place[item]
        owner = 2 * plane_of(item) + core
        px = piece(full, owner, item[1], seq if mine else xn)
        py = piece(full, owner, item[1], seq if mine else yn)
        return (remote(px, px, px_send.at[i], px_recv.at[i], (doc, xn)),
                remote(py, py, py_send.at[i], py_recv.at[i], (doc, yn)))

    def diagonal_copies(item, mine):
        i = place[item]
        owner = 2 * plane_of(item) + core
        top = piece(full, owner, item[1], xn if mine else dn, 0, rows // 2)
        low = piece(full, owner, item[1], yn if mine else dn, rows // 2, rows // 2)
        return (remote(top, top, dx_send.at[i], dx_recv.at[i], (doc, yn)),
                remote(low, low, dy_send.at[i], dy_recv.at[i], (doc, xn)))

    def sibling_copy(item, which, mine):
        i = place[item]
        owner = 2 * plane_of(item) + (core if mine else 1 - core)
        spot = piece(full, owner, item[1], (seq, xn, yn, dn, None)[which])
        return remote(spot, spot, sib_send.at[i * 5 + which], sib_recv.at[i * 5 + which], sibling)

    first = [(0, u, side) for u in range(SUBS) for side in range(2)]
    for item in first:
        @pl.when(onward(item))
        def _(item=item):
            line_copy(item).start()
    halo_copy = remote(tail, halo, halo_send, halo_recv, (doc, follower))
    halo_copy.start()
    own_copy = remote(shard, full.at[doc], own_send, own_recv, sibling)
    own_copy.start()
    fetch = pltpu.make_async_copy(shard, bounce, local_sem)
    fetch.start()
    fetch.wait()
    local_copy = pltpu.make_async_copy(bounce, full.at[doc], local_sem)
    local_copy.start()

    lag_plane, lag_diag = LAG_PLANE, LAG_DIAG
    for step in range(len(items) + max(lag_diag, LAG_COMMON)):
        if step == LAG_COMMON:
            for item in first:
                @pl.when(onward(item))
                def _(item=item):
                    common_copy(item).start()
        if step < len(items):
            item = items[step]

            @pl.when(exists(item))
            def _(item=item):
                line_arrival(item).wait_recv()
                if item[0] + 1 < planes:
                    @pl.when(onward(item))
                    def _():
                        line_copy(item).start()
                for copy in plane_copies(item, True):
                    copy.start()
                sibling_copy(item, 0, True).start()
        if 0 <= step - lag_plane < len(items):
            item = items[step - lag_plane]

            @pl.when(exists(item))
            def _(item=item):
                arrivals = plane_copies(item, False)
                onwards = diagonal_copies(item, True)
                for which in range(2):
                    arrivals[which].wait_recv()
                    onwards[which].start()
                    sibling_copy(item, 1 + which, True).start()
        if 0 <= step - lag_diag < len(items):
            item = items[step - lag_diag]

            @pl.when(exists(item))
            def _(item=item):
                for copy in diagonal_copies(item, False):
                    copy.wait_recv()
                sibling_copy(item, 3, True).start()
        if 0 <= step - LAG_COMMON < len(items):
            item = items[step - LAG_COMMON]

            @pl.when(exists(item))
            def _(item=item):
                common_arrival(item).wait_recv()
                if item[0] + 1 < planes:
                    @pl.when(onward(item))
                    def _():
                        common_copy(item).start()
                sibling_copy(item, 4, True).start()

    for item in first:
        @pl.when(onward(item))
        def _(item=item):
            line_copy(item).wait_send()
            common_copy(item).wait_send()
    for item in items:
        @pl.when(exists(item))
        def _(item=item):
            if item[0] + 1 < planes:
                @pl.when(onward(item))
                def _():
                    line_copy(item).wait_send()
                    common_copy(item).wait_send()
            for copy in plane_copies(item, True) + diagonal_copies(item, True):
                copy.wait_send()
            for which in range(5):
                sibling_copy(item, which, True).wait_send()
                sibling_copy(item, which, False).wait_recv()
    halo_copy.wait()
    remote(shard, full.at[doc + 1 - 2 * core], own_send, own_recv, sibling).wait()
    local_copy.wait()


def gather_weights(in_weight, tokens):
    docs = lax.axis_size("doc")
    depth, width = in_weight.shape
    if lax.axis_size("seq") != 4 or docs % 2 or docs < 4 or depth % (SUBS * 32) or width % 4096:
        full = lax.all_gather(in_weight, "doc", axis=0, tiled=True)
        count = lax.axis_size("seq")
        tail = tokens[0, tokens.shape[1] - HALO :]
        halo = lax.ppermute(tail, "seq", [(i, (i + 1) % count) for i in range(count)])
        return full, halo
    planes = docs // 2
    count = (planes - 1) * SUBS * 2
    dma = pltpu.SemaphoreType.DMA
    full, halo = pl.pallas_call(
        functools.partial(gather_kernel, planes),
        out_shape=(jax.ShapeDtypeStruct((docs, depth, width), in_weight.dtype),
                   jax.ShapeDtypeStruct((HALO, tokens.shape[2]), tokens.dtype)),
        in_specs=[HBM, HBM],
        out_specs=(HBM, HBM),
        scratch_shapes=[dma, dma, dma, dma, dma] + [dma((count,))] * 12 + [dma((count * 5,))] * 2
        + [pltpu.VMEM(in_weight.shape, in_weight.dtype)],
        compiler_params=pltpu.CompilerParams(collective_id=0, has_side_effects=True),
        name="gather_weights",
    )(in_weight, tokens)
    return full.reshape(docs * depth, width), halo


def exchange_kernel(count, state, decay, states, decays, local_sem, send_sem, recv_sem):
    doc = lax.axis_index("doc")
    seq = lax.axis_index("seq")
    barrier = pltpu.get_barrier_semaphore()
    for offset in range(1, count):
        peer = lax.rem(seq + offset, count)
        pl.semaphore_signal(barrier, inc=1, device_id=(doc, peer), device_id_type=MESH)
    pl.semaphore_wait(barrier, count - 1)

    def copies(offset, mine):
        peer = seq + offset
        place = seq if mine else seq - offset
        return [
            pltpu.make_async_remote_copy(
                src_ref=source, dst_ref=target.at[place], send_sem=send_sem.at[offset, i],
                recv_sem=recv_sem.at[offset, i], device_id=(doc, peer), device_id_type=MESH)
            for i, (source, target) in enumerate(((decay, decays), (state, states)))]

    for offset in range(1, count):
        @pl.when(seq + offset < count)
        def _(offset=offset):
            for copy in copies(offset, True):
                copy.start()
    for place in range(count):
        @pl.when(place >= seq)
        def _(place=place):
            states[place] = jnp.zeros_like(state)
            decays[place] = jnp.zeros_like(decay)
    for offset in range(1, count):
        @pl.when(seq + offset < count)
        def _(offset=offset):
            for copy in copies(offset, True):
                copy.wait_send()

        @pl.when(seq - offset >= 0)
        def _(offset=offset):
            for copy in copies(offset, False):
                copy.wait_recv()


def exchange_states(state, decay):
    count = lax.axis_size("seq")
    dma = pltpu.SemaphoreType.DMA
    return pl.pallas_call(
        functools.partial(exchange_kernel, count),
        out_shape=(jax.ShapeDtypeStruct((count,) + state.shape, state.dtype),
                   jax.ShapeDtypeStruct((count,) + decay.shape, decay.dtype)),
        in_specs=[ONCHIP, ONCHIP],
        out_specs=(ONCHIP, ONCHIP),
        scratch_shapes=[dma, dma((count, 2)), dma((count, 2))],
        compiler_params=pltpu.CompilerParams(collective_id=1, has_side_effects=True),
        name="exchange_states",
    )(state, decay)


def selector(heads, head_width, first_channel, width):
    row = lax.broadcasted_iota(jnp.int32, (2 * heads, width), 0)
    channel = first_channel + lax.broadcasted_iota(jnp.int32, (2 * heads, width), 1)
    head = lax.div(channel, head_width)
    return jnp.where((row == head) | (row == head + heads), 1.0, 0.0).astype(jnp.bfloat16)


def spread(pair, picks):
    return jnp.dot(pair, picks, preferred_element_type=jnp.float32)


def split_rows(value):
    high = value.astype(jnp.bfloat16)
    low = (value - high.astype(jnp.float32)).astype(jnp.bfloat16)
    return high, low


def project_kernel(head_width, tokens, halo, gain, weight, taps, bias, state_weight, rise, middle,
                   activated, maps, state, normed, padded):
    step = pl.program_id(0)
    first_seq = lax.axis_index("seq") == 0
    rows, inner = activated.shape
    width = weight.shape[1]

    def norm(block):
        values = block.astype(jnp.float32)
        inverse = lax.rsqrt(jnp.mean(values * values, axis=-1, keepdims=True) + 1e-05)
        return values * inverse * gain[...]

    @pl.when(step == 0)
    def _():
        kept = jnp.where(first_seq, 0.0, 1.0)
        normed[:HALO] = (norm(halo[...]) * kept).astype(jnp.bfloat16)
        normed[HALO:] = norm(tokens[...]).astype(jnp.bfloat16)
        maps[...] = jnp.zeros_like(maps)

    projected = jnp.dot(normed[...], weight[...], preferred_element_type=jnp.float32)
    padded[...] = projected.astype(jnp.bfloat16).astype(jnp.float32)
    count = taps.shape[0]
    total = jnp.zeros((rows, width), jnp.float32) + bias[...]
    for k in range(count):
        start = HALO - (count - 1) + k
        total = total + taps[k : k + 1, :] * padded[start : start + rows]
    active = (total / (1.0 + jnp.exp(-total))).astype(jnp.bfloat16)
    activated[:, pl.ds(pl.multiple_of(step * width, width), width)] = active
    maps[...] += jnp.dot(active, state_weight[...], preferred_element_type=jnp.float32)

    @pl.when(step == pl.num_programs(0) - 1)
    def _():
        entries = state.shape[0]
        turned = maps[...].T
        for group in range(inner // width):
            columns = slice(group * width, (group + 1) * width)
            carried = jnp.zeros((entries, width), jnp.float32)
            picks = selector(rise.shape[1] // 2, head_width, group * width, width)
            halves = spread(middle[...], picks)
            for block in range(rows // BLOCK):
                span = slice(block * BLOCK, (block + 1) * BLOCK)
                factor = spread(rise[span, :], picks)
                scaled = (activated[span, columns].astype(jnp.float32) * factor).astype(jnp.bfloat16)
                high, low = split_rows(turned[:entries, span])
                fresh = jnp.dot(high, scaled, preferred_element_type=jnp.float32)
                fresh = fresh + jnp.dot(low, scaled, preferred_element_type=jnp.float32)
                half = halves[block : block + 1]
                carried = half * (fresh + half * carried)
            state[:, columns] = carried.astype(jnp.bfloat16)


def scan_kernel(head_width, activated, maps, incoming, rise, fall, middle, skip, result, left):
    rows, width = activated.shape
    entries = incoming.shape[0]
    blocks = rows // BLOCK

    @pl.when(pl.program_id(0) == 0)
    def _():
        row = lax.broadcasted_iota(jnp.int32, (BLOCK, BLOCK), 0)
        column = lax.broadcasted_iota(jnp.int32, (BLOCK, BLOCK), 1)
        turned = maps[...].T
        for block in range(blocks):
            span = slice(block * BLOCK, (block + 1) * BLOCK)
            reads = maps[span, entries:]
            writes = turned[:entries, span]
            scores = jnp.dot(reads, writes, precision=lax.Precision.HIGHEST)
            left[block, :BLOCK] = jnp.where(row >= column, scores, 0.0).astype(jnp.bfloat16)
            high, low = split_rows(writes)
            left[block, BLOCK : BLOCK + entries] = high
            left[block, BLOCK + entries :] = low

    first_channel = pl.program_id(0) * width
    picks = selector(rise.shape[1] // 2, head_width, first_channel, width)
    halves = spread(middle[...], picks)
    carried = incoming[...]
    for block in range(blocks):
        span = slice(block * BLOCK, (block + 1) * BLOCK)
        values = activated[span, :].astype(jnp.float32)
        scaled = (values * spread(rise[span, :], picks)).astype(jnp.bfloat16)
        both = jnp.dot(left[block], scaled, preferred_element_type=jnp.float32)
        half = halves[block : block + 1]
        entering = half * carried
        reads = maps[span, entries:].astype(jnp.bfloat16)
        emitted = both[:BLOCK] + jnp.dot(
            reads, entering.astype(jnp.bfloat16), preferred_element_type=jnp.float32)
        emitted = emitted * spread(fall[span, :], picks)
        result[span, :] = (emitted + skip[...] * values).astype(jnp.bfloat16)
        carried = half * (both[BLOCK : BLOCK + entries] + both[BLOCK + entries :] + entering)


GROUP = 512
SHARED = 128
UNIT = 256
CHUNK = 1024
LEAD = 2
LAG_TURN = 2
LAG_SHARE = 4
LAG_WORK = 2
FAR = pl.BlockSpec(memory_space=pltpu.HBM)


def fused_kernel(head_width, shard, tokens_in, gain_in, taps_in, bias_in, state_in, retention_in, skip_in, result,
                 weights, tokens, halo, normed, padded, activated, scaled, local, gain, taps, bias, state_weight,
                 retention, skip, picks, rise, fall, reach, halves, shares, maps, left, state, states, decay, decays,
                 emitted,
                 load_sem, halo_sem, own_send, line_recv, fwd_send, px_send, px_recv, py_send, py_recv, dx_send,
                 dx_recv, dy_send, dy_recv, sib_send, sib_recv, own_local, decay_sem, state_send, state_recv, out_sem):
    doc = lax.axis_index("doc")
    seq = lax.axis_index("seq")
    z = lax.div(doc, 2)
    core = lax.rem(doc, 2)
    depth, inner = shard.shape
    rows, features = tokens.shape
    groups = inner // GROUP
    quarter = depth // 4
    entries = state.shape[1]
    blocks = rows // BLOCK
    chunks = inner // CHUNK
    xn = seq + 1 - 2 * lax.rem(seq, 2)
    yn = lax.rem(seq + 2, 4)
    dn = 3 - seq
    follower = lax.rem(seq + 1, 4)
    sibling = (doc + 1 - 2 * core, seq)
    mid = jnp.logical_or(z == 1, z == 2)
    upper = lax.div(z, 2)
    partner = z + 1 - 2 * lax.rem(z, 2)
    other = jnp.where(mid, 3 - z, z)
    planes = (partner, 2 - upper, 3 - 3 * upper)

    barrier = pltpu.get_barrier_semaphore()
    for peer in (xn, yn, dn):
        pl.semaphore_signal(barrier, inc=1, device_id=(doc, peer), device_id_type=MESH)
    pl.semaphore_signal(barrier, inc=1, device_id=sibling, device_id_type=MESH)
    pl.semaphore_signal(barrier, inc=1, device_id=(2 * partner + core, seq), device_id_type=MESH)

    @pl.when(mid)
    def _():
        pl.semaphore_signal(barrier, inc=1, device_id=(2 * other + core, seq), device_id_type=MESH)

    pl.semaphore_wait(barrier, 5 + jnp.where(mid, 1, 0))

    def remote(source, target, send, recv, device):
        return pltpu.make_async_remote_copy(
            src_ref=source, dst_ref=target, send_sem=send, recv_sem=recv,
            device_id=device, device_id_type=MESH)

    def span(start, count, unit):
        return pl.ds(pl.multiple_of(start, unit), count)

    def mine(m):
        return 2 * planes[m] + core

    def width(m):
        return GROUP - SHARED if m == 0 else GROUP

    def piece(group, owner, part, start, count, columns):
        return weights.at[group, owner, span(part * quarter + start, count, 16), pl.ds(0, columns)]

    def own_copies(group):
        at = span(part_start, quarter, 16)
        toward = (2 * partner + core, seq)
        across = (2 * other + core, seq)
        close = remote(shard.at[at, span(group * GROUP, GROUP - SHARED, LANES)],
                       piece(group, doc, seq, 0, quarter, GROUP - SHARED),
                       own_send.at[group, 0], line_recv.at[group, 0], toward)
        common = remote(shard.at[:, span(group * GROUP + GROUP - SHARED, SHARED, LANES)],
                        weights.at[group, doc, :, pl.ds(GROUP - SHARED, SHARED)],
                        own_send.at[group, 1], line_recv.at[group, 3], toward)
        beyond = remote(shard.at[at, span(group * GROUP, GROUP, LANES)],
                        piece(group, doc, seq, 0, quarter, GROUP),
                        own_send.at[group, 2], line_recv.at[group, 1], across)
        beside = remote(shard.at[:, span(group * GROUP, GROUP, LANES)], weights.at[group, doc],
                        own_send.at[group, 3], sib_recv.at[group, 3], sibling)
        here = pltpu.make_async_copy(shard.at[:, span(group * GROUP, GROUP, LANES)], weights.at[group, doc],
                                     own_local.at[group])
        return close, common, beyond, beside, here

    part_start = seq * quarter

    def start_own(group):
        close, common, beyond, beside, here = own_copies(group)
        close.start()

        @pl.when(mid)
        def _():
            beyond.start()
        common.start()
        beside.start()
        here.start()

    def line_arrivals(group, m):
        spot = piece(group, mine(m), seq, 0, quarter, width(m))
        found = [remote(spot, spot, own_send.at[group, 0], line_recv.at[group, m], sibling)]
        if m == 0:
            spot = weights.at[group, mine(m), :, pl.ds(GROUP - SHARED, SHARED)]
            found.append(remote(spot, spot, own_send.at[group, 1], line_recv.at[group, 3], sibling))
        return found

    def forward_copy(group, m):
        spot = piece(group, mine(m), seq, 0, quarter, GROUP)
        plane = other if m == 0 else partner
        return remote(spot, spot, fwd_send.at[group, m], line_recv.at[group, 2 if m == 0 else m],
                      (2 * plane + core, seq))

    def plane_copies(group, m, sent):
        px = piece(group, mine(m), seq if sent else xn, 0, quarter, width(m))
        py = piece(group, mine(m), seq if sent else yn, 0, quarter, width(m))
        return (remote(px, px, px_send.at[group, m], px_recv.at[group, m], (doc, xn)),
                remote(py, py, py_send.at[group, m], py_recv.at[group, m], (doc, yn)))

    def diagonal_copies(group, m, sent):
        top = piece(group, mine(m), xn if sent else dn, 0, quarter // 2, width(m))
        low = piece(group, mine(m), yn if sent else dn, quarter // 2, quarter // 2, width(m))
        return (remote(top, top, dx_send.at[group, m], dx_recv.at[group, m], (doc, yn)),
                remote(low, low, dy_send.at[group, m], dy_recv.at[group, m], (doc, xn)))

    def sibling_copy(group, m, sent):
        spot = weights.at[group, 2 * planes[m] + (core if sent else 1 - core)]
        return remote(spot, spot, sib_send.at[group, m], sib_recv.at[group, m], sibling)

    def arrive(group, m):
        for copy in line_arrivals(group, m):
            copy.wait_recv()

        @pl.when(mid)
        def _():
            forward_copy(group, m).start()
        for copy in plane_copies(group, m, True):
            copy.start()

    def turn(group, m):
        arrivals = plane_copies(group, m, False)
        onwards = diagonal_copies(group, m, True)
        for which in range(2):
            arrivals[which].wait_recv()
            onwards[which].start()

    def share(group, m):
        for copy in diagonal_copies(group, m, False):
            copy.wait_recv()
        sibling_copy(group, m, True).start()

    def collect(group):
        for m in range(3):
            sibling_copy(group, m, False).wait_recv()
        copies = own_copies(group)
        spot = weights.at[group, doc + 1 - 2 * core]
        remote(spot, spot, own_send.at[group, 3], sib_recv.at[group, 3], sibling).wait_recv()
        copies[4].wait()

    def settle(group):
        close, common, beyond, beside, _ = own_copies(group)
        close.wait_send()
        common.wait_send()
        beside.wait_send()

        @pl.when(mid)
        def _():
            beyond.wait_send()
            for m in range(3):
                forward_copy(group, m).wait_send()
        for m in range(3):
            for copy in plane_copies(group, m, True) + diagonal_copies(group, m, True):
                copy.wait_send()
            sibling_copy(group, m, True).wait_send()

    for group in range(LEAD):
        start_own(group)
    tail = tokens_in.at[pl.ds(rows - HALO, HALO)]
    halo_copy = remote(tail, halo, halo_sem.at[0], halo_sem.at[1], (doc, follower))
    halo_copy.start()
    heads = retention_in.shape[0]
    loads = [pltpu.make_async_copy(source, target, load_sem.at[i]) for i, (source, target) in enumerate((
        (tokens_in, tokens), (gain_in, gain), (taps_in, taps), (bias_in, bias), (state_in, state_weight),
        (skip_in, skip), (retention_in, retention.at[pl.ds(0, heads)]),
        (retention_in, retention.at[pl.ds(heads, heads)])))]
    for load in loads:
        load.start()

    def pairs(value):
        lane = lax.broadcasted_iota(jnp.int32, value.shape, 1)
        high = value.astype(jnp.bfloat16).astype(jnp.float32)
        return jnp.where(lane < heads, high, value - high).astype(jnp.bfloat16)

    def norm(block):
        values = block.astype(jnp.float32)
        inverse = lax.rsqrt(jnp.mean(values * values, axis=-1, keepdims=True) + 1e-05)
        return values * inverse * gain[...]

    def sent_decay(offset):
        return remote(decay, decays.at[seq], decay_sem.at[0, offset], decay_sem.at[1, offset], (doc, seq + offset))

    def got_decay(offset):
        return remote(decay, decays.at[seq - offset], decay_sem.at[0, offset], decay_sem.at[1, offset], sibling)

    def prepare():
        for load in loads:
            load.wait()
        maps[...] = jnp.zeros_like(maps)
        for place in range(4):
            @pl.when(place >= seq)
            def _(place=place):
                states[place] = jnp.zeros(states.shape[1:], states.dtype)
                decays[place] = jnp.zeros(decays.shape[1:], decays.dtype)
        row = lax.broadcasted_iota(jnp.int32, (BLOCK, BLOCK), 0)
        column = lax.broadcasted_iota(jnp.int32, (BLOCK, BLOCK), 1)
        lower = jnp.where(row >= column, 1.0, 0.0)
        logs = jnp.log(retention[...]).T
        before = jnp.zeros((1, LANES), jnp.float32)
        place = lax.broadcasted_iota(jnp.int32, (HALO, LANES), 0)
        half = jnp.zeros((HALO, LANES), jnp.float32)
        for block in range(blocks):
            part = slice(block * BLOCK, (block + 1) * BLOCK)
            within = jnp.dot(lower, logs[part], precision=lax.Precision.HIGHEST)
            end = within[BLOCK - 1 : BLOCK]
            rise[part] = pairs(jnp.exp(0.5 * end - within))
            fall[part] = pairs(jnp.exp(within - 0.5 * end))
            reach[part] = pairs(jnp.exp(before + within))
            half = jnp.where(place == block, jnp.exp(0.5 * end), half)
            before = before + end
        decay[...] = jnp.broadcast_to(before, decay.shape)
        for offset in range(1, 4):
            @pl.when(seq + offset < 4)
            def _(offset=offset):
                sent_decay(offset).start()
        for chunk in range(chunks):
            at = slice(chunk * CHUNK, (chunk + 1) * CHUNK)
            picks[:, at] = selector(heads, head_width, chunk * CHUNK, CHUNK)
            halves[:, at] = jnp.dot(pairs(half), picks[:, at], preferred_element_type=jnp.float32)

        def norm_rows(i, _):
            part = span(i * 64, 64, 64)
            normed[span(HALO + i * 64, 64, 16)] = norm(tokens[part]).astype(jnp.bfloat16)
            return 0
        lax.fori_loop(0, rows // 64, norm_rows, 0)
        halo_copy.wait()
        kept = jnp.where(seq == 0, 0.0, 1.0)
        normed[:HALO] = (norm(halo[...]) * kept).astype(jnp.bfloat16)

    def weigh():
        for offset in range(1, 4):
            @pl.when(seq + offset < 4)
            def _(offset=offset):
                sent_decay(offset).wait_send()

            @pl.when(seq - offset >= 0)
            def _(offset=offset):
                got_decay(offset).wait_recv()
        place = lax.broadcasted_iota(jnp.int32, (HALO, LANES), 0)
        total = jnp.zeros((HALO, LANES), jnp.float32)
        for later in range(1, 4):
            log = jnp.where(later < seq, decays[later][:1], 0.0)
            total = total + jnp.where(place < later, log, 0.0)
        share_of = pairs(jnp.where(place < seq, jnp.exp(total), 0.0))
        for chunk in range(chunks):
            at = slice(chunk * CHUNK, (chunk + 1) * CHUNK)
            shares[:, at] = jnp.dot(share_of, picks[:, at], preferred_element_type=jnp.float32)

    def work(group, unit):
        at = pl.ds(unit * UNIT, UNIT)
        block = weights[group, :, :, at].reshape(features, UNIT)
        projected = jnp.dot(normed[...], block, preferred_element_type=jnp.float32)
        padded[...] = projected.astype(jnp.bfloat16).astype(jnp.float32)
        columns = span(group * GROUP + unit * UNIT, UNIT, UNIT)
        count = taps.shape[0]
        total = jnp.zeros((rows, UNIT), jnp.float32) + bias[:, columns]
        for k in range(count):
            start = HALO - (count - 1) + k
            total = total + taps[k : k + 1, columns] * padded[start : start + rows]
        active = (total / (1.0 + jnp.exp(-total))).astype(jnp.bfloat16)
        activated[:, columns] = active
        maps[...] += lax.dot_general(active, state_weight[:, columns], (((1,), (1,)), ((), ())),
                                     preferred_element_type=jnp.float32)
        factor = jnp.dot(rise[...], picks[:, columns], preferred_element_type=jnp.float32)
        scaled[:, columns] = (active.astype(jnp.float32) * factor).astype(jnp.bfloat16)

    def within_groups(group):
        return jnp.logical_and(group >= 0, group < groups)

    def step(t, _):
        for m in range(3):
            @pl.when(t < groups)
            def _():
                arrive(t, m)
            for lag, action in ((LAG_TURN, turn), (LAG_SHARE, share)):
                back, which = (lag + 2 - m) // 3, (m - lag) % 3

                @pl.when(within_groups(t - back))
                def _():
                    action(t - back, which)
            if m == 0:
                @pl.when(t + LEAD < groups)
                def _():
                    start_own(t + LEAD)

                @pl.when(t == 0)
                def _():
                    prepare()

                @pl.when(t == 2)
                def _():
                    weigh()

                @pl.when(within_groups(t - LAG_WORK))
                def _():
                    collect(t - LAG_WORK)
            if m > 0:
                @pl.when(within_groups(t - LAG_WORK))
                def _():
                    work(t - LAG_WORK, m - 1)
        @pl.when(within_groups(t - LAG_WORK))
        def _():
            settle(t - LAG_WORK)
        return 0

    lax.fori_loop(0, groups + LAG_WORK, step, 0)

    row = lax.broadcasted_iota(jnp.int32, (BLOCK, BLOCK), 0)
    column = lax.broadcasted_iota(jnp.int32, (BLOCK, BLOCK), 1)
    turned = maps[...].T
    for block in range(blocks):
        part = slice(block * BLOCK, (block + 1) * BLOCK)
        reads = maps[part, entries:]
        writes = turned[:entries, part]
        scores = jnp.dot(reads, writes, precision=lax.Precision.HIGHEST)
        left[block, :BLOCK] = jnp.where(row >= column, scores, 0.0).astype(jnp.bfloat16)
        high, low = split_rows(writes)
        left[block, BLOCK : BLOCK + entries] = high
        left[block, BLOCK + entries :] = low

    def sent_state(chunk, offset):
        return remote(state.at[chunk], states.at[seq, chunk], state_send.at[chunk, offset],
                      state_recv.at[chunk, offset], (doc, seq + offset))

    def got_state(chunk, offset):
        return remote(state.at[chunk], states.at[seq - offset, chunk], state_send.at[chunk, offset],
                      state_recv.at[chunk, offset], sibling)

    def scan(chunk, _):
        at = span(chunk * CHUNK, CHUNK, CHUNK)
        half_of = halves[:, at]
        carried = jnp.zeros((entries, CHUNK), jnp.float32)
        for block in range(blocks):
            part = slice(block * BLOCK, (block + 1) * BLOCK)
            both = jnp.dot(left[block], scaled[part, at], preferred_element_type=jnp.float32)
            half = half_of[block : block + 1]
            entering = half * carried
            reads = maps[part, entries:].astype(jnp.bfloat16)
            value = both[:BLOCK] + jnp.dot(
                reads, entering.astype(jnp.bfloat16), preferred_element_type=jnp.float32)
            value = value * jnp.dot(fall[part], picks[:, at], preferred_element_type=jnp.float32)
            local[part, at] = value + skip[:, at] * activated[part, at].astype(jnp.float32)
            carried = half * (both[BLOCK : BLOCK + entries] + both[BLOCK + entries :] + entering)
        state[chunk] = carried.astype(jnp.bfloat16)
        for offset in range(1, 4):
            @pl.when(seq + offset < 4)
            def _(offset=offset):
                sent_state(chunk, offset).start()
        return 0

    lax.fori_loop(0, chunks, scan, 0)

    def out_copy(chunk):
        at = span(chunk * CHUNK, CHUNK, CHUNK)
        return pltpu.make_async_copy(emitted.at[:, at], result.at[:, at], out_sem.at[chunk])

    def finish(chunk, _):
        at = span(chunk * CHUNK, CHUNK, CHUNK)
        for offset in range(1, 4):
            @pl.when(seq - offset >= 0)
            def _(offset=offset):
                got_state(chunk, offset).wait_recv()
        incoming = jnp.zeros((entries, CHUNK), jnp.float32)
        for place in range(3):
            incoming = incoming + shares[place : place + 1, at] * states[place, chunk].astype(jnp.float32)
        incoming = incoming.astype(jnp.bfloat16)
        for block in range(blocks):
            part = slice(block * BLOCK, (block + 1) * BLOCK)
            reads = maps[part, entries:].astype(jnp.bfloat16)
            more = jnp.dot(reads, incoming, preferred_element_type=jnp.float32)
            factor = jnp.dot(reach[part], picks[:, at], preferred_element_type=jnp.float32)
            emitted[part, at] = (local[part, at] + factor * more).astype(jnp.bfloat16)
        out_copy(chunk).start()
        return 0

    lax.fori_loop(0, chunks, finish, 0)
    for chunk in range(chunks):
        out_copy(chunk).wait()
        for offset in range(1, 4):
            @pl.when(seq + offset < 4)
            def _(chunk=chunk, offset=offset):
                sent_state(chunk, offset).wait_send()


def fused(tokens, norm_gain, in_weight, conv_weight, conv_bias, state_weight, skip_gain, retention):
    rows, features = tokens.shape[1:]
    depth, inner = in_weight.shape
    heads = retention.shape[2]
    docs = features // depth
    entries = state_weight.shape[1] // 2
    groups, chunks, blocks = inner // GROUP, inner // CHUNK, rows // BLOCK
    dma = pltpu.SemaphoreType.DMA
    vmem = pltpu.VMEM
    bf16, f32 = jnp.bfloat16, jnp.float32
    result = pl.pallas_call(
        functools.partial(fused_kernel, inner // heads),
        out_shape=jax.ShapeDtypeStruct((rows, inner), bf16),
        in_specs=[FAR] * 8,
        out_specs=FAR,
        scratch_shapes=[
            vmem((groups, docs, depth, GROUP), bf16), vmem((rows, features), bf16), vmem((HALO, features), bf16),
            vmem((HALO + rows, features), bf16), vmem((HALO + rows, UNIT), f32), vmem((rows, inner), bf16),
            vmem((rows, inner), bf16), vmem((rows, inner), f32), vmem((1, features), f32),
            vmem(conv_weight.shape, f32), vmem((1, inner), f32), vmem((2 * entries, inner), bf16),
            vmem((2 * heads, rows), f32), vmem((1, inner), f32), vmem((2 * heads, inner), bf16),
            vmem((rows, LANES), bf16), vmem((rows, LANES), bf16), vmem((rows, LANES), bf16),
            vmem((HALO, inner), f32), vmem((HALO, inner), f32), vmem((rows, 2 * entries), f32),
            vmem((blocks, BLOCK + 2 * entries, BLOCK), bf16), vmem((chunks, entries, CHUNK), bf16),
            vmem((4, chunks, entries, CHUNK), bf16), vmem((8, LANES), f32), vmem((4, 8, LANES), f32),
            vmem((rows, inner), bf16),
            dma((8,)), dma((2,)), dma((groups, 4)), dma((groups, 4))] + [dma((groups, 3))] * 10 + [
            dma((groups, 4)), dma((groups,)), dma((2, 4)), dma((chunks, 4)), dma((chunks, 4)), dma((chunks,))],
        compiler_params=pltpu.CompilerParams(
            collective_id=2, has_side_effects=True, vmem_limit_bytes=60 * 1024 * 1024),
        name="fused",
    )(in_weight, tokens[0], norm_gain[None], conv_weight, conv_bias[None], state_weight.T, retention[0].T,
      skip_gain[None])
    return result[None]


def body(tokens, norm_gain, in_weight, conv_weight, conv_bias, state_weight, skip_gain, retention):
    rows, features = tokens.shape[1:]
    inner = in_weight.shape[1]
    heads = retention.shape[2]
    head_width = inner // heads
    entries = state_weight.shape[1] // 2
    blocks = rows // BLOCK
    steps = inner // WIDTH
    taps = conv_weight.shape[0]
    count = lax.axis_size("seq")
    seq = lax.axis_index("seq")

    if (lax.axis_size("doc") == 8 and count == 4 and in_weight.shape[0] % 64 == 0 and heads == 64 and inner % CHUNK == 0
            and rows % BLOCK == 0):
        return fused(tokens, norm_gain, in_weight, conv_weight, conv_bias, state_weight, skip_gain, retention)

    full, halo = gather_weights(in_weight, tokens)

    log_rates = jnp.log(retention[0]).reshape(blocks, BLOCK, heads)
    lower = jnp.tril(jnp.ones((BLOCK, BLOCK), jnp.float32))
    within = jnp.einsum("ij,bjh->bih", lower, log_rates, precision=lax.Precision.HIGHEST)
    ends = within[:, -1]
    middle = 0.5 * ends
    rise = jnp.exp(middle[:, None] - within).reshape(rows, heads)
    fall = jnp.exp(within - middle[:, None]).reshape(rows, heads)
    half = jnp.exp(middle)

    def paired(value):
        high = lax.reduce_precision(value, 8, 7)
        return jnp.concatenate([high, value - high], axis=1).astype(jnp.bfloat16)

    rise, fall = paired(rise), paired(fall)
    half = jnp.pad(paired(half), ((0, -blocks % 16), (0, 0)))

    whole = lambda shape: pl.BlockSpec(shape, lambda j: (0,) * len(shape))
    params = pltpu.CompilerParams(vmem_limit_bytes=48 * 1024 * 1024)
    activated, maps, state = pl.pallas_call(
        functools.partial(project_kernel, head_width),
        grid=(steps,),
        out_shape=(jax.ShapeDtypeStruct((rows, inner), jnp.bfloat16),
                   jax.ShapeDtypeStruct((rows, 2 * entries), jnp.float32),
                   jax.ShapeDtypeStruct((entries, inner), jnp.bfloat16)),
        in_specs=[
            whole((rows, features)), whole((HALO, features)), whole((1, features)),
            pl.BlockSpec((full.shape[0], WIDTH), lambda j: (0, j)),
            pl.BlockSpec((taps, WIDTH), lambda j: (0, j)),
            pl.BlockSpec((1, WIDTH), lambda j: (0, j)),
            pl.BlockSpec((WIDTH, 2 * entries), lambda j: (j, 0)),
            whole(rise.shape), whole(half.shape),
        ],
        out_specs=(whole((rows, inner)), whole((rows, 2 * entries)), whole((entries, inner))),
        scratch_shapes=[pltpu.VMEM((HALO + rows, features), jnp.bfloat16),
                        pltpu.VMEM((HALO + rows, WIDTH), jnp.float32)],
        compiler_params=params,
        name="project",
    )(tokens[0], halo, norm_gain[None], full, conv_weight, conv_bias[None], state_weight, rise,
      half)

    decay = jnp.broadcast_to(jnp.pad(jnp.sum(ends, axis=0), (0, LANES - heads)), (8, LANES))
    states, decays = exchange_states(state, decay)
    index = jnp.arange(count)
    later = (index[None, :] > index[:, None]) & (index[None, :] < seq)
    logs = jnp.sum(jnp.where(later[:, :, None], decays[None, :, 0, :heads], 0.0), axis=1)
    shares = jnp.where(index[:, None] < seq, jnp.exp(logs), 0.0)
    shares = jnp.repeat(shares, head_width, axis=1)
    incoming = jnp.sum(shares[:, None] * states.astype(jnp.float32), axis=0)

    result = pl.pallas_call(
        functools.partial(scan_kernel, head_width),
        grid=(steps,),
        out_shape=jax.ShapeDtypeStruct((rows, inner), jnp.bfloat16),
        in_specs=[
            pl.BlockSpec((rows, WIDTH), lambda j: (0, j)),
            whole((rows, 2 * entries)),
            pl.BlockSpec((entries, WIDTH), lambda j: (0, j)),
            whole(rise.shape), whole(fall.shape), whole(half.shape),
            pl.BlockSpec((1, WIDTH), lambda j: (0, j)),
        ],
        out_specs=pl.BlockSpec((rows, WIDTH), lambda j: (0, j)),
        scratch_shapes=[pltpu.VMEM((blocks, BLOCK + 2 * entries, BLOCK), jnp.bfloat16)],
        compiler_params=params,
        name="scan",
    )(activated, maps, incoming, rise, fall, half, skip_gain[None])
    return result[None]


def solution(mesh):
    return jax.shard_map(
        body,
        mesh=mesh,
        in_specs=(
            P("doc", "seq", None),
            P(),
            P("doc", None),
            P(),
            P(),
            P(),
            P(),
            P("doc", "seq", None),
        ),
        out_specs=P("doc", "seq", None),
        check_vma=False,
    )
```

```python
import functools
import jax
import jax.numpy as jnp
from jax import lax
from jax.experimental import pallas as pl
from jax.experimental.pallas import tpu as pltpu
from jax.sharding import PartitionSpec as P

BLOCK = 128
LANES = 128
HALO = 16
WIDTH = 2048
SUBS = 2
COMMON = 8
LAG_PLANE = 3
LAG_DIAG = 6
LAG_COMMON = 4
MESH = pl.DeviceIdType.MESH
HBM = pl.BlockSpec(memory_space=pl.ANY)
ONCHIP = pl.BlockSpec(memory_space=pltpu.VMEM)


def gather_kernel(planes, shard, tokens, full, halo, local_sem, own_send, own_recv, halo_send,
                  halo_recv, line_send, line_recv, px_send, px_recv, py_send, py_recv, dx_send,
                  dx_recv, dy_send, dy_recv, com_send, com_recv,
                  sib_send, sib_recv, bounce):
    doc = lax.axis_index("doc")
    seq = lax.axis_index("seq")
    z = lax.div(doc, 2)
    core = lax.rem(doc, 2)
    depth, width = shard.shape
    common = width // COMMON
    quarter = (width - common) // 4
    rows = depth // SUBS
    tail = tokens.at[0, pl.ds(tokens.shape[1] - HALO, HALO)]
    xn = seq + 1 - 2 * lax.rem(seq, 2)
    yn = lax.rem(seq + 2, 4)
    dn = 3 - seq
    follower = lax.rem(seq + 1, 4)
    leader = lax.rem(seq + 3, 4)
    sibling = (doc + 1 - 2 * core, seq)

    barrier = pltpu.get_barrier_semaphore()
    for peer in (xn, yn, dn):
        pl.semaphore_signal(barrier, inc=1, device_id=(doc, peer), device_id_type=MESH)
    pl.semaphore_signal(barrier, inc=1, device_id=sibling, device_id_type=MESH)

    @pl.when(z > 0)
    def _():
        pl.semaphore_signal(barrier, inc=1, device_id=(doc - 2, seq), device_id_type=MESH)

    @pl.when(z < planes - 1)
    def _():
        pl.semaphore_signal(barrier, inc=1, device_id=(doc + 2, seq), device_id_type=MESH)

    ends = jnp.where(z > 0, 1, 0) + jnp.where(z < planes - 1, 1, 0)
    pl.semaphore_wait(barrier, 4 + ends)

    def piece(ref, owner, sub, column, start=0, count=rows):
        if column is None:
            columns = pl.ds(4 * quarter, common)
        else:
            columns = pl.ds(pl.multiple_of(column * quarter, LANES), quarter)
        if owner is None:
            return ref.at[pl.ds(sub * rows + start, count), columns]
        return ref.at[owner, pl.ds(sub * rows + start, count), columns]

    def remote(source, target, send, recv, device):
        return pltpu.make_async_remote_copy(
            src_ref=source, dst_ref=target, send_sem=send, recv_sem=recv,
            device_id=device, device_id_type=MESH)

    items = [(k, u, side) for k in range(1, planes) for u in range(SUBS) for side in range(2)]
    place = {item: i for i, item in enumerate(items)}

    def plane_of(item):
        return z - item[0] if item[2] == 0 else z + item[0]

    def exists(item):
        return plane_of(item) >= 0 if item[2] == 0 else plane_of(item) < planes

    def onward(item):
        there = z < planes - 1 if item[2] == 0 else z > 0
        return jnp.logical_and(exists(item), there) if item[0] > 0 else there

    def line_copy(item):
        i = place[(item[0] + 1, item[1], item[2])]
        owner = 2 * plane_of(item) + core
        target = piece(full, owner, item[1], seq)
        source = piece(shard, None, item[1], seq) if item[0] == 0 else target
        device = (doc + 2, seq) if item[2] == 0 else (doc - 2, seq)
        return remote(source, target, line_send.at[i], line_recv.at[i], device)

    def common_copy(item):
        i = place[(item[0] + 1, item[1], item[2])]
        owner = 2 * plane_of(item) + core
        target = piece(full, owner, item[1], None)
        source = piece(shard, None, item[1], None) if item[0] == 0 else target
        device = (doc + 2, seq) if item[2] == 0 else (doc - 2, seq)
        return remote(source, target, com_send.at[i], com_recv.at[i], device)

    def common_arrival(item):
        i = place[item]
        target = piece(full, 2 * plane_of(item) + core, item[1], None)
        return remote(target, target, com_send.at[i], com_recv.at[i], sibling)

    def line_arrival(item):
        i = place[item]
        target = piece(full, 2 * plane_of(item) + core, item[1], seq)
        return remote(target, target, line_send.at[i], line_recv.at[i], sibling)

    def plane_copies(item, mine):
        i = place[item]
        owner = 2 * plane_of(item) + core
        px = piece(full, owner, item[1], seq if mine else xn)
        py = piece(full, owner, item[1], seq if mine else yn)
        return (remote(px, px, px_send.at[i], px_recv.at[i], (doc, xn)),
                remote(py, py, py_send.at[i], py_recv.at[i], (doc, yn)))

    def diagonal_copies(item, mine):
        i = place[item]
        owner = 2 * plane_of(item) + core
        top = piece(full, owner, item[1], xn if mine else dn, 0, rows // 2)
        low = piece(full, owner, item[1], yn if mine else dn, rows // 2, rows // 2)
        return (remote(top, top, dx_send.at[i], dx_recv.at[i], (doc, yn)),
                remote(low, low, dy_send.at[i], dy_recv.at[i], (doc, xn)))

    def sibling_copy(item, which, mine):
        i = place[item]
        owner = 2 * plane_of(item) + (core if mine else 1 - core)
        spot = piece(full, owner, item[1], (seq, xn, yn, dn, None)[which])
        return remote(spot, spot, sib_send.at[i * 5 + which], sib_recv.at[i * 5 + which], sibling)

    first = [(0, u, side) for u in range(SUBS) for side in range(2)]
    for item in first:
        @pl.when(onward(item))
        def _(item=item):
            line_copy(item).start()
    halo_copy = remote(tail, halo, halo_send, halo_recv, (doc, follower))
    halo_copy.start()
    own_copy = remote(shard, full.at[doc], own_send, own_recv, sibling)
    own_copy.start()
    fetch = pltpu.make_async_copy(shard, bounce, local_sem)
    fetch.start()
    fetch.wait()
    local_copy = pltpu.make_async_copy(bounce, full.at[doc], local_sem)
    local_copy.start()

    lag_plane, lag_diag = LAG_PLANE, LAG_DIAG
    for step in range(len(items) + max(lag_diag, LAG_COMMON)):
        if step == LAG_COMMON:
            for item in first:
                @pl.when(onward(item))
                def _(item=item):
                    common_copy(item).start()
        if step < len(items):
            item = items[step]

            @pl.when(exists(item))
            def _(item=item):
                line_arrival(item).wait_recv()
                if item[0] + 1 < planes:
                    @pl.when(onward(item))
                    def _():
                        line_copy(item).start()
                for copy in plane_copies(item, True):
                    copy.start()
                sibling_copy(item, 0, True).start()
        if 0 <= step - lag_plane < len(items):
            item = items[step - lag_plane]

            @pl.when(exists(item))
            def _(item=item):
                arrivals = plane_copies(item, False)
                onwards = diagonal_copies(item, True)
                for which in range(2):
                    arrivals[which].wait_recv()
                    onwards[which].start()
                    sibling_copy(item, 1 + which, True).start()
        if 0 <= step - lag_diag < len(items):
            item = items[step - lag_diag]

            @pl.when(exists(item))
            def _(item=item):
                for copy in diagonal_copies(item, False):
                    copy.wait_recv()
                sibling_copy(item, 3, True).start()
        if 0 <= step - LAG_COMMON < len(items):
            item = items[step - LAG_COMMON]

            @pl.when(exists(item))
            def _(item=item):
                common_arrival(item).wait_recv()
                if item[0] + 1 < planes:
                    @pl.when(onward(item))
                    def _():
                        common_copy(item).start()
                sibling_copy(item, 4, True).start()

    for item in first:
        @pl.when(onward(item))
        def _(item=item):
            line_copy(item).wait_send()
            common_copy(item).wait_send()
    for item in items:
        @pl.when(exists(item))
        def _(item=item):
            if item[0] + 1 < planes:
                @pl.when(onward(item))
                def _():
                    line_copy(item).wait_send()
                    common_copy(item).wait_send()
            for copy in plane_copies(item, True) + diagonal_copies(item, True):
                copy.wait_send()
            for which in range(5):
                sibling_copy(item, which, True).wait_send()
                sibling_copy(item, which, False).wait_recv()
    halo_copy.wait()
    remote(shard, full.at[doc + 1 - 2 * core], own_send, own_recv, sibling).wait()
    local_copy.wait()


def gather_weights(in_weight, tokens):
    docs = lax.axis_size("doc")
    depth, width = in_weight.shape
    if lax.axis_size("seq") != 4 or docs % 2 or docs < 4 or depth % (SUBS * 32) or width % 4096:
        full = lax.all_gather(in_weight, "doc", axis=0, tiled=True)
        count = lax.axis_size("seq")
        tail = tokens[0, tokens.shape[1] - HALO :]
        halo = lax.ppermute(tail, "seq", [(i, (i + 1) % count) for i in range(count)])
        return full, halo
    planes = docs // 2
    count = (planes - 1) * SUBS * 2
    dma = pltpu.SemaphoreType.DMA
    full, halo = pl.pallas_call(
        functools.partial(gather_kernel, planes),
        out_shape=(jax.ShapeDtypeStruct((docs, depth, width), in_weight.dtype),
                   jax.ShapeDtypeStruct((HALO, tokens.shape[2]), tokens.dtype)),
        in_specs=[HBM, HBM],
        out_specs=(HBM, HBM),
        scratch_shapes=[dma, dma, dma, dma, dma] + [dma((count,))] * 12 + [dma((count * 5,))] * 2
        + [pltpu.VMEM(in_weight.shape, in_weight.dtype)],
        compiler_params=pltpu.CompilerParams(collective_id=0, has_side_effects=True),
        name="gather_weights",
    )(in_weight, tokens)
    return full.reshape(docs * depth, width), halo


def exchange_kernel(count, state, decay, states, decays, local_sem, send_sem, recv_sem):
    doc = lax.axis_index("doc")
    seq = lax.axis_index("seq")
    barrier = pltpu.get_barrier_semaphore()
    for offset in range(1, count):
        peer = lax.rem(seq + offset, count)
        pl.semaphore_signal(barrier, inc=1, device_id=(doc, peer), device_id_type=MESH)
    pl.semaphore_wait(barrier, count - 1)

    def copies(offset, mine):
        peer = seq + offset
        place = seq if mine else seq - offset
        return [
            pltpu.make_async_remote_copy(
                src_ref=source, dst_ref=target.at[place], send_sem=send_sem.at[offset, i],
                recv_sem=recv_sem.at[offset, i], device_id=(doc, peer), device_id_type=MESH)
            for i, (source, target) in enumerate(((decay, decays), (state, states)))]

    for offset in range(1, count):
        @pl.when(seq + offset < count)
        def _(offset=offset):
            for copy in copies(offset, True):
                copy.start()
    for place in range(count):
        @pl.when(place >= seq)
        def _(place=place):
            states[place] = jnp.zeros_like(state)
            decays[place] = jnp.zeros_like(decay)
    for offset in range(1, count):
        @pl.when(seq + offset < count)
        def _(offset=offset):
            for copy in copies(offset, True):
                copy.wait_send()

        @pl.when(seq - offset >= 0)
        def _(offset=offset):
            for copy in copies(offset, False):
                copy.wait_recv()


def exchange_states(state, decay):
    count = lax.axis_size("seq")
    dma = pltpu.SemaphoreType.DMA
    return pl.pallas_call(
        functools.partial(exchange_kernel, count),
        out_shape=(jax.ShapeDtypeStruct((count,) + state.shape, state.dtype),
                   jax.ShapeDtypeStruct((count,) + decay.shape, decay.dtype)),
        in_specs=[ONCHIP, ONCHIP],
        out_specs=(ONCHIP, ONCHIP),
        scratch_shapes=[dma, dma((count, 2)), dma((count, 2))],
        compiler_params=pltpu.CompilerParams(collective_id=1, has_side_effects=True),
        name="exchange_states",
    )(state, decay)


def selector(heads, head_width, first_channel, width):
    row = lax.broadcasted_iota(jnp.int32, (2 * heads, width), 0)
    channel = first_channel + lax.broadcasted_iota(jnp.int32, (2 * heads, width), 1)
    start = jnp.where(row < heads, row, row - heads) * head_width
    return jnp.where((channel >= start) & (channel < start + head_width), 1.0, 0.0).astype(jnp.bfloat16)


def spread(pair, picks):
    return jnp.dot(pair, picks, preferred_element_type=jnp.float32)


def split_rows(value):
    high = value.astype(jnp.bfloat16)
    low = (value - high.astype(jnp.float32)).astype(jnp.bfloat16)
    return high, low


def project_kernel(head_width, tokens, halo, gain, weight, taps, bias, state_weight, rise, middle,
                   activated, maps, state, normed, padded):
    step = pl.program_id(0)
    first_seq = lax.axis_index("seq") == 0
    rows, inner = activated.shape
    width = weight.shape[1]

    def norm(block):
        values = block.astype(jnp.float32)
        inverse = lax.rsqrt(jnp.mean(values * values, axis=-1, keepdims=True) + 1e-05)
        return values * inverse * gain[...]

    @pl.when(step == 0)
    def _():
        kept = jnp.where(first_seq, 0.0, 1.0)
        normed[:HALO] = (norm(halo[...]) * kept).astype(jnp.bfloat16)
        normed[HALO:] = norm(tokens[...]).astype(jnp.bfloat16)
        maps[...] = jnp.zeros_like(maps)

    projected = jnp.dot(normed[...], weight[...], preferred_element_type=jnp.float32)
    padded[...] = projected.astype(jnp.bfloat16).astype(jnp.float32)
    count = taps.shape[0]
    total = jnp.zeros((rows, width), jnp.float32) + bias[...]
    for k in range(count):
        start = HALO - (count - 1) + k
        total = total + taps[k : k + 1, :] * padded[start : start + rows]
    active = (total / (1.0 + jnp.exp(-total))).astype(jnp.bfloat16)
    activated[:, pl.ds(pl.multiple_of(step * width, width), width)] = active
    maps[...] += jnp.dot(active, state_weight[...], preferred_element_type=jnp.float32)

    @pl.when(step == pl.num_programs(0) - 1)
    def _():
        entries = state.shape[0]
        turned = maps[...].T
        for group in range(inner // width):
            columns = slice(group * width, (group + 1) * width)
            carried = jnp.zeros((entries, width), jnp.float32)
            picks = selector(rise.shape[1] // 2, head_width, group * width, width)
            halves = spread(middle[...], picks)
            for block in range(rows // BLOCK):
                span = slice(block * BLOCK, (block + 1) * BLOCK)
                factor = spread(rise[span, :], picks)
                scaled = (activated[span, columns].astype(jnp.float32) * factor).astype(jnp.bfloat16)
                high, low = split_rows(turned[:entries, span])
                fresh = jnp.dot(high, scaled, preferred_element_type=jnp.float32)
                fresh = fresh + jnp.dot(low, scaled, preferred_element_type=jnp.float32)
                half = halves[block : block + 1]
                carried = half * (fresh + half * carried)
            state[:, columns] = carried.astype(jnp.bfloat16)


def scan_kernel(head_width, activated, maps, incoming, rise, fall, middle, skip, result, left):
    rows, width = activated.shape
    entries = incoming.shape[0]
    blocks = rows // BLOCK

    @pl.when(pl.program_id(0) == 0)
    def _():
        row = lax.broadcasted_iota(jnp.int32, (BLOCK, BLOCK), 0)
        column = lax.broadcasted_iota(jnp.int32, (BLOCK, BLOCK), 1)
        turned = maps[...].T
        for block in range(blocks):
            span = slice(block * BLOCK, (block + 1) * BLOCK)
            reads = maps[span, entries:]
            writes = turned[:entries, span]
            scores = jnp.dot(reads, writes, precision=lax.Precision.HIGHEST)
            left[block, :BLOCK] = jnp.where(row >= column, scores, 0.0).astype(jnp.bfloat16)
            high, low = split_rows(writes)
            left[block, BLOCK : BLOCK + entries] = high
            left[block, BLOCK + entries :] = low

    first_channel = pl.program_id(0) * width
    picks = selector(rise.shape[1] // 2, head_width, first_channel, width)
    halves = spread(middle[...], picks)
    carried = incoming[...]
    for block in range(blocks):
        span = slice(block * BLOCK, (block + 1) * BLOCK)
        values = activated[span, :].astype(jnp.float32)
        scaled = (values * spread(rise[span, :], picks)).astype(jnp.bfloat16)
        both = jnp.dot(left[block], scaled, preferred_element_type=jnp.float32)
        half = halves[block : block + 1]
        entering = half * carried
        reads = maps[span, entries:].astype(jnp.bfloat16)
        emitted = both[:BLOCK] + jnp.dot(
            reads, entering.astype(jnp.bfloat16), preferred_element_type=jnp.float32)
        emitted = emitted * spread(fall[span, :], picks)
        result[span, :] = (emitted + skip[...] * values).astype(jnp.bfloat16)
        carried = half * (both[BLOCK : BLOCK + entries] + both[BLOCK + entries :] + entering)


GROUP = 512
SHARED = 128
UNIT = 256
CHUNK = 1024
LEAD_END = 3
LEAD_CLOSE = 2
LEAD_COMMON = 0
FIRST = 0
LEAD_BEYOND = 2
LEAD_LOCAL = 2
LAG_TURN = 3
LAG_SHARE = 6
LAG_WORK = 3
FAR = pl.BlockSpec(memory_space=pltpu.HBM)


def fused_kernel(head_width, shard, tokens_in, gain_in, taps_in, bias_in, state_in, retention_in, skip_in, result,
                 weights, tokens, halo, normed, padded, activated, scaled,
                 local, gain, taps, bias, state_weight, retention, skip, picks, rise, fall, reach, halves, shares,
                 maps, reads, across, falls, reaches, left, state, states, emitted, decay, decays, load_sem, halo_sem, own_send, line_recv, fwd_send, px_send, px_recv, py_send, py_recv, dx_send,
                 dx_recv, dy_send, dy_recv, sib_send, sib_recv, own_local, decay_sem, state_send, state_recv, out_sem):
    doc = lax.axis_index("doc")
    seq = lax.axis_index("seq")
    z = lax.div(doc, 2)
    core = lax.rem(doc, 2)
    depth, inner = shard.shape
    rows, features = tokens.shape
    groups = inner // GROUP
    quarter = depth // 4
    entries = state.shape[1]
    blocks = rows // BLOCK
    chunks = inner // CHUNK
    xn = seq + 1 - 2 * lax.rem(seq, 2)
    yn = lax.rem(seq + 2, 4)
    dn = 3 - seq
    follower = lax.rem(seq + 1, 4)
    sibling = (doc + 1 - 2 * core, seq)
    mid = jnp.logical_or(z == 1, z == 2)
    upper = lax.div(z, 2)
    partner = z + 1 - 2 * lax.rem(z, 2)
    other = jnp.where(mid, 3 - z, z)
    planes = (partner, 2 - upper, 3 - 3 * upper)

    barrier = pltpu.get_barrier_semaphore()
    for peer in (xn, yn, dn):
        pl.semaphore_signal(barrier, inc=1, device_id=(doc, peer), device_id_type=MESH)
    pl.semaphore_signal(barrier, inc=1, device_id=sibling, device_id_type=MESH)
    pl.semaphore_signal(barrier, inc=1, device_id=(2 * partner + core, seq), device_id_type=MESH)

    @pl.when(mid)
    def _():
        pl.semaphore_signal(barrier, inc=1, device_id=(2 * other + core, seq), device_id_type=MESH)

    pl.semaphore_wait(barrier, 5 + jnp.where(mid, 1, 0))

    def remote(source, target, send, recv, device):
        return pltpu.make_async_remote_copy(
            src_ref=source, dst_ref=target, send_sem=send, recv_sem=recv,
            device_id=device, device_id_type=MESH)

    def span(start, count, unit):
        return pl.ds(pl.multiple_of(start, unit), count)

    def mine(m):
        return 2 * planes[m] + core

    def width(m):
        return GROUP - SHARED if m == 0 else GROUP

    def piece(group, owner, part, start, count, columns):
        return weights.at[group, owner, span(part * quarter + start, count, 16), pl.ds(0, columns)]

    def own_copies(group):
        at = span(part_start, quarter, 16)
        toward = (2 * partner + core, seq)
        across = (2 * other + core, seq)
        close = remote(shard.at[at, span(group * GROUP, GROUP - SHARED, LANES)],
                       piece(group, doc, seq, 0, quarter, GROUP - SHARED),
                       own_send.at[group, 0], line_recv.at[group, 0], toward)
        common = remote(shard.at[:, span(group * GROUP + GROUP - SHARED, SHARED, LANES)],
                        weights.at[group, doc, :, pl.ds(GROUP - SHARED, SHARED)],
                        own_send.at[group, 1], line_recv.at[group, 3], toward)
        beyond = remote(shard.at[at, span(group * GROUP, GROUP, LANES)],
                        piece(group, doc, seq, 0, quarter, GROUP),
                        own_send.at[group, 2], line_recv.at[group, 1], across)
        beside = remote(shard.at[:, span(group * GROUP, GROUP, LANES)], weights.at[group, doc],
                        own_send.at[group, 3], sib_recv.at[group, 3], sibling)
        here = pltpu.make_async_copy(shard.at[:, span(group * GROUP, GROUP, LANES)], weights.at[group, doc],
                                     own_local.at[group])
        return close, common, beyond, beside, here

    part_start = seq * quarter

    def start_close(group):
        own_copies(group)[0].start()

    def start_common(group):
        own_copies(group)[1].start()

    def start_beyond(group):
        own_copies(group)[2].start()

    def start_local(group):
        own_copies(group)[3].start()
        own_copies(group)[4].start()

    def line_arrival(group, m):
        spot = piece(group, mine(m), seq, 0, quarter, width(m))
        return remote(spot, spot, own_send.at[group, 0], line_recv.at[group, m], sibling)

    def common_arrival(group):
        spot = weights.at[group, mine(0), :, pl.ds(GROUP - SHARED, SHARED)]
        return remote(spot, spot, own_send.at[group, 1], line_recv.at[group, 3], sibling)

    def forward_copy(group, m):
        spot = piece(group, mine(m), seq, 0, quarter, GROUP)
        plane = other if m == 0 else partner
        return remote(spot, spot, fwd_send.at[group, m], line_recv.at[group, 2 if m == 0 else m],
                      (2 * plane + core, seq))

    def plane_copies(group, m, sent):
        px = piece(group, mine(m), seq if sent else xn, 0, quarter, width(m))
        py = piece(group, mine(m), seq if sent else yn, 0, quarter, width(m))
        return (remote(px, px, px_send.at[group, m], px_recv.at[group, m], (doc, xn)),
                remote(py, py, py_send.at[group, m], py_recv.at[group, m], (doc, yn)))

    def diagonal_copies(group, m, sent):
        top = piece(group, mine(m), xn if sent else dn, 0, quarter // 2, width(m))
        low = piece(group, mine(m), yn if sent else dn, quarter // 2, quarter // 2, width(m))
        return (remote(top, top, dx_send.at[group, m], dx_recv.at[group, m], (doc, yn)),
                remote(low, low, dy_send.at[group, m], dy_recv.at[group, m], (doc, xn)))

    def sibling_copy(group, m, sent):
        spot = weights.at[group, 2 * planes[m] + (core if sent else 1 - core)]
        return remote(spot, spot, sib_send.at[group, m], sib_recv.at[group, m], sibling)

    def arrive(group, m):
        line_arrival(group, m).wait_recv()

        @pl.when(mid)
        def _():
            if m == 0:
                common_arrival(group).wait_recv()
            forward_copy(group, m).start()
        for copy in plane_copies(group, m, True):
            copy.start()

    def turn(group, m):
        arrivals = plane_copies(group, m, False)
        onwards = diagonal_copies(group, m, True)
        for which in range(2):
            arrivals[which].wait_recv()
            onwards[which].start()

    def share(group, m):
        for copy in diagonal_copies(group, m, False):
            copy.wait_recv()
        if m == 0:
            @pl.when(edge)
            def _():
                common_arrival(group).wait_recv()
        sibling_copy(group, m, True).start()

    def collect(group):
        for m in range(3):
            sibling_copy(group, m, False).wait_recv()
        copies = own_copies(group)
        spot = weights.at[group, doc + 1 - 2 * core]
        remote(spot, spot, own_send.at[group, 3], sib_recv.at[group, 3], sibling).wait_recv()
        copies[4].wait()

    def settle(group):
        close, common, beyond, beside, _ = own_copies(group)
        close.wait_send()
        common.wait_send()
        beside.wait_send()

        @pl.when(mid)
        def _():
            beyond.wait_send()
            for m in range(3):
                forward_copy(group, m).wait_send()
        for m in range(3):
            for copy in plane_copies(group, m, True) + diagonal_copies(group, m, True):
                copy.wait_send()
            sibling_copy(group, m, True).wait_send()

    edge = jnp.logical_not(mid)
    def start_both(group):
        start_close(group)
        start_common(group)

    leads = ((start_both, edge, LEAD_END), (start_close, mid, LEAD_CLOSE),
             (start_common, mid, LEAD_COMMON),
             (start_beyond, mid, LEAD_BEYOND), (start_local, None, LEAD_LOCAL))
    for start, needed, lead in leads:
        for group in range(lead - FIRST):
            if needed is None:
                start(group)
            else:
                pl.when(needed)(functools.partial(start, group))
    tail = tokens_in.at[pl.ds(rows - HALO, HALO)]
    halo_copy = remote(tail, halo, halo_sem.at[0], halo_sem.at[1], (doc, follower))
    halo_copy.start()
    heads = retention_in.shape[0]
    loads = [pltpu.make_async_copy(source, target, load_sem.at[i]) for i, (source, target) in enumerate((
        (tokens_in, tokens), (gain_in, gain), (taps_in, taps), (bias_in, bias), (state_in, state_weight),
        (skip_in, skip), (retention_in, retention.at[pl.ds(0, heads)]),
        (retention_in, retention.at[pl.ds(heads, heads)])))]
    for load in loads:
        load.start()

    def pairs(value):
        lane = lax.broadcasted_iota(jnp.int32, value.shape, 1)
        high = value.astype(jnp.bfloat16).astype(jnp.float32)
        return jnp.where(lane < heads, high, value - high).astype(jnp.bfloat16)

    def norm(block):
        values = block.astype(jnp.float32)
        inverse = lax.rsqrt(jnp.mean(values * values, axis=-1, keepdims=True) + 1e-05)
        return values * inverse * gain[...]

    def sent_decay(offset):
        return remote(decay, decays.at[seq], decay_sem.at[0, offset], decay_sem.at[1, offset], (doc, seq + offset))

    def got_decay(offset):
        return remote(decay, decays.at[seq - offset], decay_sem.at[0, offset], decay_sem.at[1, offset], sibling)

    def prepare():
        for load in loads:
            load.wait()
        maps[...] = jnp.zeros_like(maps)
        for place in range(4):
            @pl.when(place >= seq)
            def _(place=place):
                states[place] = jnp.zeros(states.shape[1:], states.dtype)
                decays[place] = jnp.zeros(decays.shape[1:], decays.dtype)
        row = lax.broadcasted_iota(jnp.int32, (BLOCK, BLOCK), 0)
        column = lax.broadcasted_iota(jnp.int32, (BLOCK, BLOCK), 1)
        lower = jnp.where(row >= column, 1.0, 0.0)
        logs = jnp.log(retention[...]).T
        before = jnp.zeros((1, LANES), jnp.float32)
        place = lax.broadcasted_iota(jnp.int32, (HALO, LANES), 0)
        half = jnp.zeros((HALO, LANES), jnp.float32)
        for block in range(blocks):
            part = slice(block * BLOCK, (block + 1) * BLOCK)
            within = jnp.dot(lower, logs[part], precision=lax.Precision.HIGHEST)
            end = within[BLOCK - 1 : BLOCK]
            rise[part] = pairs(jnp.exp(0.5 * end - within))
            fall[part] = pairs(jnp.exp(within - 0.5 * end))
            reach[part] = pairs(jnp.exp(before + within))
            half = jnp.where(place == block, jnp.exp(0.5 * end), half)
            before = before + end
        decay[...] = jnp.broadcast_to(before, decay.shape)
        for offset in range(1, 4):
            @pl.when(seq + offset < 4)
            def _(offset=offset):
                sent_decay(offset).start()
        for chunk in range(chunks):
            at = slice(chunk * CHUNK, (chunk + 1) * CHUNK)
            picks[:, at] = selector(heads, head_width, chunk * CHUNK, CHUNK)
            halves[:, at] = jnp.dot(pairs(half), picks[:, at], preferred_element_type=jnp.float32)

        def norm_rows(i, _):
            part = span(i * 64, 64, 64)
            normed[span(HALO + i * 64, 64, 16)] = norm(tokens[part]).astype(jnp.bfloat16)
            return 0
        lax.fori_loop(0, rows // 64, norm_rows, 0)
        halo_copy.wait()
        kept = jnp.where(seq == 0, 0.0, 1.0)
        normed[:HALO] = (norm(halo[...]) * kept).astype(jnp.bfloat16)

    def weigh():
        for offset in range(1, 4):
            @pl.when(seq + offset < 4)
            def _(offset=offset):
                sent_decay(offset).wait_send()

            @pl.when(seq - offset >= 0)
            def _(offset=offset):
                got_decay(offset).wait_recv()
        place = lax.broadcasted_iota(jnp.int32, (HALO, LANES), 0)
        total = jnp.zeros((HALO, LANES), jnp.float32)
        for later in range(1, 4):
            log = jnp.where(later < seq, decays[later][:1], 0.0)
            total = total + jnp.where(place < later, log, 0.0)
        share_of = pairs(jnp.where(place < seq, jnp.exp(total), 0.0))
        for chunk in range(chunks):
            at = slice(chunk * CHUNK, (chunk + 1) * CHUNK)
            shares[:, at] = jnp.dot(share_of, picks[:, at], preferred_element_type=jnp.float32)

    def work(group, unit):
        at = pl.ds(unit * UNIT, UNIT)
        block = weights[group, :, :, at].reshape(features, UNIT)
        projected = jnp.dot(normed[...], block, preferred_element_type=jnp.float32)
        padded[...] = projected.astype(jnp.bfloat16).astype(jnp.float32)
        columns = span(group * GROUP + unit * UNIT, UNIT, UNIT)
        count = taps.shape[0]
        total = jnp.zeros((rows, UNIT), jnp.float32) + bias[:, columns]
        for k in range(count):
            start = HALO - (count - 1) + k
            total = total + taps[k : k + 1, columns] * padded[start : start + rows]
        active = (total / (1.0 + jnp.exp(-total))).astype(jnp.bfloat16)
        activated[:, columns] = active
        maps[...] += lax.dot_general(active, state_weight[:, columns], (((1,), (1,)), ((), ())),
                                     preferred_element_type=jnp.float32)
        reaches[:, columns] = jnp.dot(reach[...], picks[:, columns], preferred_element_type=jnp.float32)
        falls[:, columns] = jnp.dot(fall[...], picks[:, columns], preferred_element_type=jnp.float32)
        factor = jnp.dot(rise[...], picks[:, columns], preferred_element_type=jnp.float32)
        scaled[:, columns] = (active.astype(jnp.float32) * factor).astype(jnp.bfloat16)

    def within_groups(group):
        return jnp.logical_and(group >= 0, group < groups)

    def step(t, _):
        for m in range(3):
            ahead = FIRST if m == 0 else 0

            @pl.when(within_groups(t + ahead))
            def _():
                arrive(t + ahead, m)
            for lag, action in ((LAG_TURN, turn), (LAG_SHARE, share)):
                back, which = (lag + 2 - m) // 3, (m - lag) % 3
                back = back - FIRST if which == 0 else back

                @pl.when(within_groups(t - back))
                def _():
                    action(t - back, which)
            if m == 0:
                for start, needed, lead in leads:
                    on = within_groups(t + lead)
                    on = on if needed is None else jnp.logical_and(needed, on)

                    @pl.when(on)
                    def _():
                        start(t + lead)

                @pl.when(t == -FIRST)
                def _():
                    prepare()

                @pl.when(t == 2)
                def _():
                    weigh()

                @pl.when(within_groups(t - LAG_WORK))
                def _():
                    collect(t - LAG_WORK)
            if m > 0:
                @pl.when(within_groups(t - LAG_WORK))
                def _():
                    work(t - LAG_WORK, m - 1)
        @pl.when(within_groups(t - LAG_WORK))
        def _():
            settle(t - LAG_WORK)
        return 0

    lax.fori_loop(-FIRST, groups + LAG_WORK, step, 0)

    reads[...] = maps[:, entries:].astype(jnp.bfloat16)
    across[...] = jnp.zeros_like(across)
    for block in range(1, blocks):
        across[(block - 1) * BLOCK : block * BLOCK, (block - 1) * entries : block * entries] = (
            maps[block * BLOCK : (block + 1) * BLOCK, entries:].astype(jnp.bfloat16))
    row = lax.broadcasted_iota(jnp.int32, (BLOCK, BLOCK), 0)
    column = lax.broadcasted_iota(jnp.int32, (BLOCK, BLOCK), 1)
    turned = maps[...].T
    for block in range(blocks):
        part = slice(block * BLOCK, (block + 1) * BLOCK)
        writes = turned[:entries, part]
        scores = jnp.dot(maps[part, entries:], writes, precision=lax.Precision.HIGHEST)
        left[block, :BLOCK] = jnp.where(row >= column, scores, 0.0).astype(jnp.bfloat16)
        high, low = split_rows(writes)
        left[block, BLOCK : BLOCK + entries] = high
        left[block, BLOCK + entries :] = low

    def sent_state(chunk, offset):
        return remote(state.at[chunk], states.at[seq, chunk], state_send.at[chunk, offset],
                      state_recv.at[chunk, offset], (doc, seq + offset))

    def got_state(chunk, offset):
        return remote(state.at[chunk], states.at[seq - offset, chunk], state_send.at[chunk, offset],
                      state_recv.at[chunk, offset], sibling)

    def scan(chunk, _):
        at = span(chunk * CHUNK, CHUNK, CHUNK)
        half_of = halves[:, at]
        carried = jnp.zeros((entries, CHUNK), jnp.float32)
        inside, enter = [], []
        for block in range(blocks):
            part = slice(block * BLOCK, (block + 1) * BLOCK)
            both = jnp.dot(left[block], scaled[part, at], preferred_element_type=jnp.float32)
            half = half_of[block : block + 1]
            entering = half * carried
            inside.append(both[:BLOCK])
            enter.append(entering.astype(jnp.bfloat16))
            carried = half * (both[BLOCK : BLOCK + entries] + both[BLOCK + entries :] + entering)
        state[chunk] = carried.astype(jnp.bfloat16)
        crossed = jnp.dot(across[...], jnp.concatenate(enter[1:], axis=0), preferred_element_type=jnp.float32)
        for block in range(blocks):
            part = slice(block * BLOCK, (block + 1) * BLOCK)
            value = inside[block]
            if block > 0:
                value = value + crossed[(block - 1) * BLOCK : block * BLOCK]
            value = value * falls[part, at] + skip[:, at] * activated[part, at].astype(jnp.float32)
            local[chunk, part] = value
        for offset in range(1, 4):
            @pl.when(seq + offset < 4)
            def _(offset=offset):
                sent_state(chunk, offset).start()
        return 0

    lax.fori_loop(0, chunks, scan, 0)
    def out_copy(chunk):
        return pltpu.make_async_copy(emitted.at[chunk], result.at[chunk], out_sem.at[chunk])

    def finish(chunk, _):
        at = span(chunk * CHUNK, CHUNK, CHUNK)
        for offset in range(1, 4):
            @pl.when(seq - offset >= 0)
            def _(offset=offset):
                got_state(chunk, offset).wait_recv()
        incoming = jnp.zeros((entries, CHUNK), jnp.float32)
        for place in range(3):
            incoming = incoming + shares[place : place + 1, at] * states[place, chunk].astype(jnp.float32)
        more = jnp.dot(reads[...], incoming.astype(jnp.bfloat16), preferred_element_type=jnp.float32)
        emitted[chunk] = (local[chunk] + reaches[:, at] * more).astype(jnp.bfloat16)
        out_copy(chunk).start()
        return 0

    lax.fori_loop(0, chunks, finish, 0)
    for chunk in range(chunks):
        out_copy(chunk).wait()
        for offset in range(1, 4):
            @pl.when(seq + offset < 4)
            def _(chunk=chunk, offset=offset):
                sent_state(chunk, offset).wait_send()


def place_kernel(source, result, held, load_sem, out_sem):
    chunks, _, width = source.shape
    loads = [pltpu.make_async_copy(source.at[i], held.at[i], load_sem.at[i]) for i in range(chunks)]
    stores = [pltpu.make_async_copy(held.at[i], result.at[:, pl.ds(i * width, width)], out_sem.at[i])
              for i in range(chunks)]
    for copy in loads:
        copy.start()
    for load, store in zip(loads, stores):
        load.wait()
        store.start()
    for copy in stores:
        copy.wait()


def fused(tokens, norm_gain, in_weight, conv_weight, conv_bias, state_weight, skip_gain, retention):
    rows, features = tokens.shape[1:]
    depth, inner = in_weight.shape
    heads = retention.shape[2]
    docs = features // depth
    entries = state_weight.shape[1] // 2
    groups, chunks, blocks = inner // GROUP, inner // CHUNK, rows // BLOCK
    dma = pltpu.SemaphoreType.DMA
    vmem = pltpu.VMEM
    bf16, f32 = jnp.bfloat16, jnp.float32
    shape = jax.ShapeDtypeStruct
    emitted = pl.pallas_call(
        functools.partial(fused_kernel, inner // heads),
        out_shape=shape((chunks, rows, CHUNK), bf16),
        in_specs=[FAR] * 8,
        out_specs=FAR,
        scratch_shapes=[
            vmem((groups, docs, depth, GROUP), bf16), vmem((rows, features), bf16), vmem((HALO, features), bf16),
            vmem((HALO + rows, features), bf16), vmem((HALO + rows, UNIT), f32), vmem((rows, inner), bf16),
            vmem((rows, inner), bf16), vmem((chunks, rows, CHUNK), f32), vmem((1, features), f32),
            vmem(conv_weight.shape, f32), vmem((1, inner), f32), vmem((2 * entries, inner), bf16),
            vmem((2 * heads, rows), f32), vmem((1, inner), f32), vmem((2 * heads, inner), bf16),
            vmem((rows, LANES), bf16), vmem((rows, LANES), bf16), vmem((rows, LANES), bf16),
            vmem((HALO, inner), f32), vmem((HALO, inner), f32), vmem((rows, 2 * entries), f32),
            vmem((rows, entries), bf16), vmem((rows - BLOCK, (blocks - 1) * entries), bf16), vmem((rows, inner), f32),
            vmem((rows, inner), f32), vmem((blocks, BLOCK + 2 * entries, BLOCK), bf16),
            vmem((chunks, entries, CHUNK), bf16), vmem((4, chunks, entries, CHUNK), bf16),
            vmem((chunks, rows, CHUNK), bf16), vmem((8, LANES), f32), vmem((4, 8, LANES), f32),
            dma((8,)), dma((2,)), dma((groups, 4)), dma((groups, 4))] + [dma((groups, 3))] * 10 + [
            dma((groups, 4)), dma((groups,)), dma((2, 4)), dma((chunks, 4)), dma((chunks, 4)), dma((chunks,))],
        compiler_params=pltpu.CompilerParams(
            collective_id=2, has_side_effects=True, vmem_limit_bytes=60 * 1024 * 1024),
        name="fused",
    )(in_weight, tokens[0], norm_gain[None], conv_weight, conv_bias[None], state_weight.T, retention[0].T,
      skip_gain[None])
    result = pl.pallas_call(
        place_kernel,
        out_shape=shape((rows, inner), bf16),
        in_specs=[FAR],
        out_specs=FAR,
        scratch_shapes=[vmem(emitted.shape, bf16), dma((chunks,)), dma((chunks,))],
        compiler_params=pltpu.CompilerParams(vmem_limit_bytes=60 * 1024 * 1024),
        name="place",
    )(emitted)
    return result[None]


def body(tokens, norm_gain, in_weight, conv_weight, conv_bias, state_weight, skip_gain, retention):
    rows, features = tokens.shape[1:]
    inner = in_weight.shape[1]
    heads = retention.shape[2]
    head_width = inner // heads
    entries = state_weight.shape[1] // 2
    blocks = rows // BLOCK
    steps = inner // WIDTH
    taps = conv_weight.shape[0]
    count = lax.axis_size("seq")
    seq = lax.axis_index("seq")

    if (lax.axis_size("doc") == 8 and count == 4 and in_weight.shape[0] % 64 == 0 and heads == 64 and inner % CHUNK == 0
            and rows % BLOCK == 0):
        return fused(tokens, norm_gain, in_weight, conv_weight, conv_bias, state_weight, skip_gain, retention)

    full, halo = gather_weights(in_weight, tokens)

    log_rates = jnp.log(retention[0]).reshape(blocks, BLOCK, heads)
    lower = jnp.tril(jnp.ones((BLOCK, BLOCK), jnp.float32))
    within = jnp.einsum("ij,bjh->bih", lower, log_rates, precision=lax.Precision.HIGHEST)
    ends = within[:, -1]
    middle = 0.5 * ends
    rise = jnp.exp(middle[:, None] - within).reshape(rows, heads)
    fall = jnp.exp(within - middle[:, None]).reshape(rows, heads)
    half = jnp.exp(middle)

    def paired(value):
        high = lax.reduce_precision(value, 8, 7)
        return jnp.concatenate([high, value - high], axis=1).astype(jnp.bfloat16)

    rise, fall = paired(rise), paired(fall)
    half = jnp.pad(paired(half), ((0, -blocks % 16), (0, 0)))

    whole = lambda shape: pl.BlockSpec(shape, lambda j: (0,) * len(shape))
    params = pltpu.CompilerParams(vmem_limit_bytes=48 * 1024 * 1024)
    activated, maps, state = pl.pallas_call(
        functools.partial(project_kernel, head_width),
        grid=(steps,),
        out_shape=(jax.ShapeDtypeStruct((rows, inner), jnp.bfloat16),
                   jax.ShapeDtypeStruct((rows, 2 * entries), jnp.float32),
                   jax.ShapeDtypeStruct((entries, inner), jnp.bfloat16)),
        in_specs=[
            whole((rows, features)), whole((HALO, features)), whole((1, features)),
            pl.BlockSpec((full.shape[0], WIDTH), lambda j: (0, j)),
            pl.BlockSpec((taps, WIDTH), lambda j: (0, j)),
            pl.BlockSpec((1, WIDTH), lambda j: (0, j)),
            pl.BlockSpec((WIDTH, 2 * entries), lambda j: (j, 0)),
            whole(rise.shape), whole(half.shape),
        ],
        out_specs=(whole((rows, inner)), whole((rows, 2 * entries)), whole((entries, inner))),
        scratch_shapes=[pltpu.VMEM((HALO + rows, features), jnp.bfloat16),
                        pltpu.VMEM((HALO + rows, WIDTH), jnp.float32)],
        compiler_params=params,
        name="project",
    )(tokens[0], halo, norm_gain[None], full, conv_weight, conv_bias[None], state_weight, rise,
      half)

    decay = jnp.broadcast_to(jnp.pad(jnp.sum(ends, axis=0), (0, LANES - heads)), (8, LANES))
    states, decays = exchange_states(state, decay)
    index = jnp.arange(count)
    later = (index[None, :] > index[:, None]) & (index[None, :] < seq)
    logs = jnp.sum(jnp.where(later[:, :, None], decays[None, :, 0, :heads], 0.0), axis=1)
    shares = jnp.where(index[:, None] < seq, jnp.exp(logs), 0.0)
    shares = jnp.repeat(shares, head_width, axis=1)
    incoming = jnp.sum(shares[:, None] * states.astype(jnp.float32), axis=0)

    result = pl.pallas_call(
        functools.partial(scan_kernel, head_width),
        grid=(steps,),
        out_shape=jax.ShapeDtypeStruct((rows, inner), jnp.bfloat16),
        in_specs=[
            pl.BlockSpec((rows, WIDTH), lambda j: (0, j)),
            whole((rows, 2 * entries)),
            pl.BlockSpec((entries, WIDTH), lambda j: (0, j)),
            whole(rise.shape), whole(fall.shape), whole(half.shape),
            pl.BlockSpec((1, WIDTH), lambda j: (0, j)),
        ],
        out_specs=pl.BlockSpec((rows, WIDTH), lambda j: (0, j)),
        scratch_shapes=[pltpu.VMEM((blocks, BLOCK + 2 * entries, BLOCK), jnp.bfloat16)],
        compiler_params=params,
        name="scan",
    )(activated, maps, incoming, rise, fall, half, skip_gain[None])
    return result[None]


def solution(mesh):
    return jax.shard_map(
        body,
        mesh=mesh,
        in_specs=(
            P("doc", "seq", None),
            P(),
            P("doc", None),
            P(),
            P(),
            P(),
            P(),
            P("doc", "seq", None),
        ),
        out_specs=P("doc", "seq", None),
        check_vma=False,
    )
```

```python
import functools
import jax
import jax.numpy as jnp
from jax import lax
from jax.experimental import pallas as pl
from jax.experimental.pallas import tpu as pltpu
from jax.sharding import PartitionSpec as P

BLOCK = 128
LANES = 128
HALO = 16
WIDTH = 2048
SUBS = 2
COMMON = 8
LAG_PLANE = 3
LAG_DIAG = 6
LAG_COMMON = 4
MESH = pl.DeviceIdType.MESH
HBM = pl.BlockSpec(memory_space=pl.ANY)
ONCHIP = pl.BlockSpec(memory_space=pltpu.VMEM)


def gather_kernel(planes, shard, tokens, full, halo, local_sem, own_send, own_recv, halo_send,
                  halo_recv, line_send, line_recv, px_send, px_recv, py_send, py_recv, dx_send,
                  dx_recv, dy_send, dy_recv, com_send, com_recv,
                  sib_send, sib_recv, bounce):
    doc = lax.axis_index("doc")
    seq = lax.axis_index("seq")
    z = lax.div(doc, 2)
    core = lax.rem(doc, 2)
    depth, width = shard.shape
    common = width // COMMON
    quarter = (width - common) // 4
    rows = depth // SUBS
    tail = tokens.at[0, pl.ds(tokens.shape[1] - HALO, HALO)]
    xn = seq + 1 - 2 * lax.rem(seq, 2)
    yn = lax.rem(seq + 2, 4)
    dn = 3 - seq
    follower = lax.rem(seq + 1, 4)
    leader = lax.rem(seq + 3, 4)
    sibling = (doc + 1 - 2 * core, seq)

    barrier = pltpu.get_barrier_semaphore()
    for peer in (xn, yn, dn):
        pl.semaphore_signal(barrier, inc=1, device_id=(doc, peer), device_id_type=MESH)
    pl.semaphore_signal(barrier, inc=1, device_id=sibling, device_id_type=MESH)

    @pl.when(z > 0)
    def _():
        pl.semaphore_signal(barrier, inc=1, device_id=(doc - 2, seq), device_id_type=MESH)

    @pl.when(z < planes - 1)
    def _():
        pl.semaphore_signal(barrier, inc=1, device_id=(doc + 2, seq), device_id_type=MESH)

    ends = jnp.where(z > 0, 1, 0) + jnp.where(z < planes - 1, 1, 0)
    pl.semaphore_wait(barrier, 4 + ends)

    def piece(ref, owner, sub, column, start=0, count=rows):
        if column is None:
            columns = pl.ds(4 * quarter, common)
        else:
            columns = pl.ds(pl.multiple_of(column * quarter, LANES), quarter)
        if owner is None:
            return ref.at[pl.ds(sub * rows + start, count), columns]
        return ref.at[owner, pl.ds(sub * rows + start, count), columns]

    def remote(source, target, send, recv, device):
        return pltpu.make_async_remote_copy(
            src_ref=source, dst_ref=target, send_sem=send, recv_sem=recv,
            device_id=device, device_id_type=MESH)

    items = [(k, u, side) for k in range(1, planes) for u in range(SUBS) for side in range(2)]
    place = {item: i for i, item in enumerate(items)}

    def plane_of(item):
        return z - item[0] if item[2] == 0 else z + item[0]

    def exists(item):
        return plane_of(item) >= 0 if item[2] == 0 else plane_of(item) < planes

    def onward(item):
        there = z < planes - 1 if item[2] == 0 else z > 0
        return jnp.logical_and(exists(item), there) if item[0] > 0 else there

    def line_copy(item):
        i = place[(item[0] + 1, item[1], item[2])]
        owner = 2 * plane_of(item) + core
        target = piece(full, owner, item[1], seq)
        source = piece(shard, None, item[1], seq) if item[0] == 0 else target
        device = (doc + 2, seq) if item[2] == 0 else (doc - 2, seq)
        return remote(source, target, line_send.at[i], line_recv.at[i], device)

    def common_copy(item):
        i = place[(item[0] + 1, item[1], item[2])]
        owner = 2 * plane_of(item) + core
        target = piece(full, owner, item[1], None)
        source = piece(shard, None, item[1], None) if item[0] == 0 else target
        device = (doc + 2, seq) if item[2] == 0 else (doc - 2, seq)
        return remote(source, target, com_send.at[i], com_recv.at[i], device)

    def common_arrival(item):
        i = place[item]
        target = piece(full, 2 * plane_of(item) + core, item[1], None)
        return remote(target, target, com_send.at[i], com_recv.at[i], sibling)

    def line_arrival(item):
        i = place[item]
        target = piece(full, 2 * plane_of(item) + core, item[1], seq)
        return remote(target, target, line_send.at[i], line_recv.at[i], sibling)

    def plane_copies(item, mine):
        i = place[item]
        owner = 2 * plane_of(item) + core
        px = piece(full, owner, item[1], seq if mine else xn)
        py = piece(full, owner, item[1], seq if mine else yn)
        return (remote(px, px, px_send.at[i], px_recv.at[i], (doc, xn)),
                remote(py, py, py_send.at[i], py_recv.at[i], (doc, yn)))

    def diagonal_copies(item, mine):
        i = place[item]
        owner = 2 * plane_of(item) + core
        top = piece(full, owner, item[1], xn if mine else dn, 0, rows // 2)
        low = piece(full, owner, item[1], yn if mine else dn, rows // 2, rows // 2)
        return (remote(top, top, dx_send.at[i], dx_recv.at[i], (doc, yn)),
                remote(low, low, dy_send.at[i], dy_recv.at[i], (doc, xn)))

    def sibling_copy(item, which, mine):
        i = place[item]
        owner = 2 * plane_of(item) + (core if mine else 1 - core)
        spot = piece(full, owner, item[1], (seq, xn, yn, dn, None)[which])
        return remote(spot, spot, sib_send.at[i * 5 + which], sib_recv.at[i * 5 + which], sibling)

    first = [(0, u, side) for u in range(SUBS) for side in range(2)]
    for item in first:
        @pl.when(onward(item))
        def _(item=item):
            line_copy(item).start()
    halo_copy = remote(tail, halo, halo_send, halo_recv, (doc, follower))
    halo_copy.start()
    own_copy = remote(shard, full.at[doc], own_send, own_recv, sibling)
    own_copy.start()
    fetch = pltpu.make_async_copy(shard, bounce, local_sem)
    fetch.start()
    fetch.wait()
    local_copy = pltpu.make_async_copy(bounce, full.at[doc], local_sem)
    local_copy.start()

    lag_plane, lag_diag = LAG_PLANE, LAG_DIAG
    for step in range(len(items) + max(lag_diag, LAG_COMMON)):
        if step == LAG_COMMON:
            for item in first:
                @pl.when(onward(item))
                def _(item=item):
                    common_copy(item).start()
        if step < len(items):
            item = items[step]

            @pl.when(exists(item))
            def _(item=item):
                line_arrival(item).wait_recv()
                if item[0] + 1 < planes:
                    @pl.when(onward(item))
                    def _():
                        line_copy(item).start()
                for copy in plane_copies(item, True):
                    copy.start()
                sibling_copy(item, 0, True).start()
        if 0 <= step - lag_plane < len(items):
            item = items[step - lag_plane]

            @pl.when(exists(item))
            def _(item=item):
                arrivals = plane_copies(item, False)
                onwards = diagonal_copies(item, True)
                for which in range(2):
                    arrivals[which].wait_recv()
                    onwards[which].start()
                    sibling_copy(item, 1 + which, True).start()
        if 0 <= step - lag_diag < len(items):
            item = items[step - lag_diag]

            @pl.when(exists(item))
            def _(item=item):
                for copy in diagonal_copies(item, False):
                    copy.wait_recv()
                sibling_copy(item, 3, True).start()
        if 0 <= step - LAG_COMMON < len(items):
            item = items[step - LAG_COMMON]

            @pl.when(exists(item))
            def _(item=item):
                common_arrival(item).wait_recv()
                if item[0] + 1 < planes:
                    @pl.when(onward(item))
                    def _():
                        common_copy(item).start()
                sibling_copy(item, 4, True).start()

    for item in first:
        @pl.when(onward(item))
        def _(item=item):
            line_copy(item).wait_send()
            common_copy(item).wait_send()
    for item in items:
        @pl.when(exists(item))
        def _(item=item):
            if item[0] + 1 < planes:
                @pl.when(onward(item))
                def _():
                    line_copy(item).wait_send()
                    common_copy(item).wait_send()
            for copy in plane_copies(item, True) + diagonal_copies(item, True):
                copy.wait_send()
            for which in range(5):
                sibling_copy(item, which, True).wait_send()
                sibling_copy(item, which, False).wait_recv()
    halo_copy.wait()
    remote(shard, full.at[doc + 1 - 2 * core], own_send, own_recv, sibling).wait()
    local_copy.wait()


def gather_weights(in_weight, tokens):
    docs = lax.axis_size("doc")
    depth, width = in_weight.shape
    if lax.axis_size("seq") != 4 or docs % 2 or docs < 4 or depth % (SUBS * 32) or width % 4096:
        full = lax.all_gather(in_weight, "doc", axis=0, tiled=True)
        count = lax.axis_size("seq")
        tail = tokens[0, tokens.shape[1] - HALO :]
        halo = lax.ppermute(tail, "seq", [(i, (i + 1) % count) for i in range(count)])
        return full, halo
    planes = docs // 2
    count = (planes - 1) * SUBS * 2
    dma = pltpu.SemaphoreType.DMA
    full, halo = pl.pallas_call(
        functools.partial(gather_kernel, planes),
        out_shape=(jax.ShapeDtypeStruct((docs, depth, width), in_weight.dtype),
                   jax.ShapeDtypeStruct((HALO, tokens.shape[2]), tokens.dtype)),
        in_specs=[HBM, HBM],
        out_specs=(HBM, HBM),
        scratch_shapes=[dma, dma, dma, dma, dma] + [dma((count,))] * 12 + [dma((count * 5,))] * 2
        + [pltpu.VMEM(in_weight.shape, in_weight.dtype)],
        compiler_params=pltpu.CompilerParams(collective_id=0, has_side_effects=True),
        name="gather_weights",
    )(in_weight, tokens)
    return full.reshape(docs * depth, width), halo


def exchange_kernel(count, state, decay, states, decays, local_sem, send_sem, recv_sem):
    doc = lax.axis_index("doc")
    seq = lax.axis_index("seq")
    barrier = pltpu.get_barrier_semaphore()
    for offset in range(1, count):
        peer = lax.rem(seq + offset, count)
        pl.semaphore_signal(barrier, inc=1, device_id=(doc, peer), device_id_type=MESH)
    pl.semaphore_wait(barrier, count - 1)

    def copies(offset, mine):
        peer = seq + offset
        place = seq if mine else seq - offset
        return [
            pltpu.make_async_remote_copy(
                src_ref=source, dst_ref=target.at[place], send_sem=send_sem.at[offset, i],
                recv_sem=recv_sem.at[offset, i], device_id=(doc, peer), device_id_type=MESH)
            for i, (source, target) in enumerate(((decay, decays), (state, states)))]

    for offset in range(1, count):
        @pl.when(seq + offset < count)
        def _(offset=offset):
            for copy in copies(offset, True):
                copy.start()
    for place in range(count):
        @pl.when(place >= seq)
        def _(place=place):
            states[place] = jnp.zeros_like(state)
            decays[place] = jnp.zeros_like(decay)
    for offset in range(1, count):
        @pl.when(seq + offset < count)
        def _(offset=offset):
            for copy in copies(offset, True):
                copy.wait_send()

        @pl.when(seq - offset >= 0)
        def _(offset=offset):
            for copy in copies(offset, False):
                copy.wait_recv()


def exchange_states(state, decay):
    count = lax.axis_size("seq")
    dma = pltpu.SemaphoreType.DMA
    return pl.pallas_call(
        functools.partial(exchange_kernel, count),
        out_shape=(jax.ShapeDtypeStruct((count,) + state.shape, state.dtype),
                   jax.ShapeDtypeStruct((count,) + decay.shape, decay.dtype)),
        in_specs=[ONCHIP, ONCHIP],
        out_specs=(ONCHIP, ONCHIP),
        scratch_shapes=[dma, dma((count, 2)), dma((count, 2))],
        compiler_params=pltpu.CompilerParams(collective_id=1, has_side_effects=True),
        name="exchange_states",
    )(state, decay)


def selector(heads, head_width, first_channel, width):
    row = lax.broadcasted_iota(jnp.int32, (2 * heads, width), 0)
    channel = first_channel + lax.broadcasted_iota(jnp.int32, (2 * heads, width), 1)
    start = jnp.where(row < heads, row, row - heads) * head_width
    return jnp.where((channel >= start) & (channel < start + head_width), 1.0, 0.0).astype(jnp.bfloat16)


def spread(pair, picks):
    return jnp.dot(pair, picks, preferred_element_type=jnp.float32)


def split_rows(value):
    high = value.astype(jnp.bfloat16)
    low = (value - high.astype(jnp.float32)).astype(jnp.bfloat16)
    return high, low


def project_kernel(head_width, tokens, halo, gain, weight, taps, bias, state_weight, rise, middle,
                   activated, maps, state, normed, padded):
    step = pl.program_id(0)
    first_seq = lax.axis_index("seq") == 0
    rows, inner = activated.shape
    width = weight.shape[1]

    def norm(block):
        values = block.astype(jnp.float32)
        inverse = lax.rsqrt(jnp.mean(values * values, axis=-1, keepdims=True) + 1e-05)
        return values * inverse * gain[...]

    @pl.when(step == 0)
    def _():
        kept = jnp.where(first_seq, 0.0, 1.0)
        normed[:HALO] = (norm(halo[...]) * kept).astype(jnp.bfloat16)
        normed[HALO:] = norm(tokens[...]).astype(jnp.bfloat16)
        maps[...] = jnp.zeros_like(maps)

    projected = jnp.dot(normed[...], weight[...], preferred_element_type=jnp.float32)
    padded[...] = projected.astype(jnp.bfloat16).astype(jnp.float32)
    count = taps.shape[0]
    total = jnp.zeros((rows, width), jnp.float32) + bias[...]
    for k in range(count):
        start = HALO - (count - 1) + k
        total = total + taps[k : k + 1, :] * padded[start : start + rows]
    active = (total / (1.0 + jnp.exp(-total))).astype(jnp.bfloat16)
    activated[:, pl.ds(pl.multiple_of(step * width, width), width)] = active
    maps[...] += jnp.dot(active, state_weight[...], preferred_element_type=jnp.float32)

    @pl.when(step == pl.num_programs(0) - 1)
    def _():
        entries = state.shape[0]
        turned = maps[...].T
        for group in range(inner // width):
            columns = slice(group * width, (group + 1) * width)
            carried = jnp.zeros((entries, width), jnp.float32)
            picks = selector(rise.shape[1] // 2, head_width, group * width, width)
            halves = spread(middle[...], picks)
            for block in range(rows // BLOCK):
                span = slice(block * BLOCK, (block + 1) * BLOCK)
                factor = spread(rise[span, :], picks)
                scaled = (activated[span, columns].astype(jnp.float32) * factor).astype(jnp.bfloat16)
                high, low = split_rows(turned[:entries, span])
                fresh = jnp.dot(high, scaled, preferred_element_type=jnp.float32)
                fresh = fresh + jnp.dot(low, scaled, preferred_element_type=jnp.float32)
                half = halves[block : block + 1]
                carried = half * (fresh + half * carried)
            state[:, columns] = carried.astype(jnp.bfloat16)


def scan_kernel(head_width, activated, maps, incoming, rise, fall, middle, skip, result, left):
    rows, width = activated.shape
    entries = incoming.shape[0]
    blocks = rows // BLOCK

    @pl.when(pl.program_id(0) == 0)
    def _():
        row = lax.broadcasted_iota(jnp.int32, (BLOCK, BLOCK), 0)
        column = lax.broadcasted_iota(jnp.int32, (BLOCK, BLOCK), 1)
        turned = maps[...].T
        for block in range(blocks):
            span = slice(block * BLOCK, (block + 1) * BLOCK)
            reads = maps[span, entries:]
            writes = turned[:entries, span]
            scores = jnp.dot(reads, writes, precision=lax.Precision.HIGHEST)
            left[block, :BLOCK] = jnp.where(row >= column, scores, 0.0).astype(jnp.bfloat16)
            high, low = split_rows(writes)
            left[block, BLOCK : BLOCK + entries] = high
            left[block, BLOCK + entries :] = low

    first_channel = pl.program_id(0) * width
    picks = selector(rise.shape[1] // 2, head_width, first_channel, width)
    halves = spread(middle[...], picks)
    carried = incoming[...]
    for block in range(blocks):
        span = slice(block * BLOCK, (block + 1) * BLOCK)
        values = activated[span, :].astype(jnp.float32)
        scaled = (values * spread(rise[span, :], picks)).astype(jnp.bfloat16)
        both = jnp.dot(left[block], scaled, preferred_element_type=jnp.float32)
        half = halves[block : block + 1]
        entering = half * carried
        reads = maps[span, entries:].astype(jnp.bfloat16)
        emitted = both[:BLOCK] + jnp.dot(
            reads, entering.astype(jnp.bfloat16), preferred_element_type=jnp.float32)
        emitted = emitted * spread(fall[span, :], picks)
        result[span, :] = (emitted + skip[...] * values).astype(jnp.bfloat16)
        carried = half * (both[BLOCK : BLOCK + entries] + both[BLOCK + entries :] + entering)


GROUP = 512
SHARED = 128
UNIT = 256
CHUNK = 1024
LEAD_END = 3
LEAD_CLOSE = 2
LEAD_COMMON = 0
FIRST = 0
LEAD_BEYOND = 2
LEAD_LOCAL = 2
LAG_TURN = 3
LAG_SHARE = 6
LAG_WORK = 3
FAR = pl.BlockSpec(memory_space=pltpu.HBM)


def fused_kernel(head_width, shard, tokens_in, gain_in, taps_in, bias_in, state_in, retention_in, skip_in, result,
                 weights, tokens, halo, normed, padded, activated, scaled,
                 local, gain, taps, bias, state_weight, retention, skip, picks, rise, fall, reach, halves, shares,
                 maps, reads, across, falls, reaches, left, state, states, emitted, decay, decays, load_sem, halo_sem, own_send, line_recv, fwd_send, px_send, px_recv, py_send, py_recv, dx_send,
                 dx_recv, dy_send, dy_recv, sib_send, sib_recv, own_local, decay_sem, state_send, state_recv, out_sem):
    doc = lax.axis_index("doc")
    seq = lax.axis_index("seq")
    z = lax.div(doc, 2)
    core = lax.rem(doc, 2)
    depth, inner = shard.shape
    rows, features = tokens.shape
    groups = inner // GROUP
    quarter = depth // 4
    entries = state.shape[1]
    blocks = rows // BLOCK
    chunks = inner // CHUNK
    xn = seq + 1 - 2 * lax.rem(seq, 2)
    yn = lax.rem(seq + 2, 4)
    dn = 3 - seq
    follower = lax.rem(seq + 1, 4)
    sibling = (doc + 1 - 2 * core, seq)
    mid = jnp.logical_or(z == 1, z == 2)
    upper = lax.div(z, 2)
    partner = z + 1 - 2 * lax.rem(z, 2)
    other = jnp.where(mid, 3 - z, z)
    planes = (partner, 2 - upper, 3 - 3 * upper)

    barrier = pltpu.get_barrier_semaphore()
    for peer in (xn, yn, dn):
        pl.semaphore_signal(barrier, inc=1, device_id=(doc, peer), device_id_type=MESH)
    pl.semaphore_signal(barrier, inc=1, device_id=sibling, device_id_type=MESH)
    pl.semaphore_signal(barrier, inc=1, device_id=(2 * partner + core, seq), device_id_type=MESH)

    @pl.when(mid)
    def _():
        pl.semaphore_signal(barrier, inc=1, device_id=(2 * other + core, seq), device_id_type=MESH)

    pl.semaphore_wait(barrier, 5 + jnp.where(mid, 1, 0))

    def remote(source, target, send, recv, device):
        return pltpu.make_async_remote_copy(
            src_ref=source, dst_ref=target, send_sem=send, recv_sem=recv,
            device_id=device, device_id_type=MESH)

    def span(start, count, unit):
        return pl.ds(pl.multiple_of(start, unit), count)

    def mine(m):
        return 2 * planes[m] + core

    def width(m):
        return GROUP - SHARED if m == 0 else GROUP

    def piece(group, owner, part, start, count, columns):
        return weights.at[group, owner, span(part * quarter + start, count, 16), pl.ds(0, columns)]

    def own_copies(group):
        at = span(part_start, quarter, 16)
        toward = (2 * partner + core, seq)
        across = (2 * other + core, seq)
        close = remote(shard.at[at, span(group * GROUP, GROUP - SHARED, LANES)],
                       piece(group, doc, seq, 0, quarter, GROUP - SHARED),
                       own_send.at[group, 0], line_recv.at[group, 0], toward)
        common = remote(shard.at[:, span(group * GROUP + GROUP - SHARED, SHARED, LANES)],
                        weights.at[group, doc, :, pl.ds(GROUP - SHARED, SHARED)],
                        own_send.at[group, 1], line_recv.at[group, 3], toward)
        beyond = remote(shard.at[at, span(group * GROUP, GROUP, LANES)],
                        piece(group, doc, seq, 0, quarter, GROUP),
                        own_send.at[group, 2], line_recv.at[group, 1], across)
        beside = remote(shard.at[:, span(group * GROUP, GROUP, LANES)], weights.at[group, doc],
                        own_send.at[group, 3], sib_recv.at[group, 3], sibling)
        here = pltpu.make_async_copy(shard.at[:, span(group * GROUP, GROUP, LANES)], weights.at[group, doc],
                                     own_local.at[group])
        return close, common, beyond, beside, here

    part_start = seq * quarter

    def start_close(group):
        own_copies(group)[0].start()

    def start_common(group):
        own_copies(group)[1].start()

    def start_beyond(group):
        own_copies(group)[2].start()

    def start_local(group):
        own_copies(group)[3].start()
        own_copies(group)[4].start()

    def line_arrival(group, m):
        spot = piece(group, mine(m), seq, 0, quarter, width(m))
        return remote(spot, spot, own_send.at[group, 0], line_recv.at[group, m], sibling)

    def common_arrival(group):
        spot = weights.at[group, mine(0), :, pl.ds(GROUP - SHARED, SHARED)]
        return remote(spot, spot, own_send.at[group, 1], line_recv.at[group, 3], sibling)

    def forward_copy(group, m):
        spot = piece(group, mine(m), seq, 0, quarter, GROUP)
        plane = other if m == 0 else partner
        return remote(spot, spot, fwd_send.at[group, m], line_recv.at[group, 2 if m == 0 else m],
                      (2 * plane + core, seq))

    def plane_copies(group, m, sent):
        px = piece(group, mine(m), seq if sent else xn, 0, quarter, width(m))
        py = piece(group, mine(m), seq if sent else yn, 0, quarter, width(m))
        return (remote(px, px, px_send.at[group, m], px_recv.at[group, m], (doc, xn)),
                remote(py, py, py_send.at[group, m], py_recv.at[group, m], (doc, yn)))

    def diagonal_copies(group, m, sent):
        top = piece(group, mine(m), xn if sent else dn, 0, quarter // 2, width(m))
        low = piece(group, mine(m), yn if sent else dn, quarter // 2, quarter // 2, width(m))
        return (remote(top, top, dx_send.at[group, m], dx_recv.at[group, m], (doc, yn)),
                remote(low, low, dy_send.at[group, m], dy_recv.at[group, m], (doc, xn)))

    def sibling_copy(group, m, sent):
        spot = weights.at[group, 2 * planes[m] + (core if sent else 1 - core)]
        return remote(spot, spot, sib_send.at[group, m], sib_recv.at[group, m], sibling)

    def arrive(group, m):
        line_arrival(group, m).wait_recv()

        @pl.when(mid)
        def _():
            if m == 0:
                common_arrival(group).wait_recv()
            forward_copy(group, m).start()
        for copy in plane_copies(group, m, True):
            copy.start()

    def turn(group, m):
        arrivals = plane_copies(group, m, False)
        onwards = diagonal_copies(group, m, True)
        for which in range(2):
            arrivals[which].wait_recv()
            onwards[which].start()

    def share(group, m):
        for copy in diagonal_copies(group, m, False):
            copy.wait_recv()
        if m == 0:
            @pl.when(edge)
            def _():
                common_arrival(group).wait_recv()
        sibling_copy(group, m, True).start()

    def collect(group):
        for m in range(3):
            sibling_copy(group, m, False).wait_recv()
        copies = own_copies(group)
        spot = weights.at[group, doc + 1 - 2 * core]
        remote(spot, spot, own_send.at[group, 3], sib_recv.at[group, 3], sibling).wait_recv()
        copies[4].wait()

    def settle(group, m):
        close, common, beyond, beside, _ = own_copies(group)
        if m == 0:
            close.wait_send()
            common.wait_send()
            beside.wait_send()

        @pl.when(mid)
        def _():
            if m == 0:
                beyond.wait_send()
            forward_copy(group, m).wait_send()
        for copy in plane_copies(group, m, True) + diagonal_copies(group, m, True):
            copy.wait_send()
        sibling_copy(group, m, True).wait_send()

    edge = jnp.logical_not(mid)
    def start_both(group):
        start_close(group)
        start_common(group)

    leads = ((start_both, edge, LEAD_END), (start_close, mid, LEAD_CLOSE),
             (start_common, mid, LEAD_COMMON),
             (start_beyond, mid, LEAD_BEYOND), (start_local, None, LEAD_LOCAL))
    for start, needed, lead in leads:
        for group in range(lead - FIRST):
            if needed is None:
                start(group)
            else:
                pl.when(needed)(functools.partial(start, group))
    tail = tokens_in.at[pl.ds(rows - HALO, HALO)]
    halo_copy = remote(tail, halo, halo_sem.at[0], halo_sem.at[1], (doc, follower))
    halo_copy.start()
    heads = retention_in.shape[0]
    loads = [pltpu.make_async_copy(source, target, load_sem.at[i]) for i, (source, target) in enumerate((
        (tokens_in, tokens), (gain_in, gain), (taps_in, taps), (bias_in, bias), (state_in, state_weight),
        (skip_in, skip), (retention_in, retention.at[pl.ds(0, heads)]),
        (retention_in, retention.at[pl.ds(heads, heads)])))]
    for load in loads:
        load.start()

    def pairs(value):
        lane = lax.broadcasted_iota(jnp.int32, value.shape, 1)
        high = value.astype(jnp.bfloat16).astype(jnp.float32)
        return jnp.where(lane < heads, high, value - high).astype(jnp.bfloat16)

    def norm(block):
        values = block.astype(jnp.float32)
        inverse = lax.rsqrt(jnp.mean(values * values, axis=-1, keepdims=True) + 1e-05)
        return values * inverse * gain[...]

    def sent_decay(offset):
        return remote(decay, decays.at[seq], decay_sem.at[0, offset], decay_sem.at[1, offset], (doc, seq + offset))

    def got_decay(offset):
        return remote(decay, decays.at[seq - offset], decay_sem.at[0, offset], decay_sem.at[1, offset], sibling)

    def prepare():
        for load in loads:
            load.wait()
        maps[...] = jnp.zeros_like(maps)
        for place in range(4):
            @pl.when(place >= seq)
            def _(place=place):
                states[place] = jnp.zeros(states.shape[1:], states.dtype)
                decays[place] = jnp.zeros(decays.shape[1:], decays.dtype)
        row = lax.broadcasted_iota(jnp.int32, (BLOCK, BLOCK), 0)
        column = lax.broadcasted_iota(jnp.int32, (BLOCK, BLOCK), 1)
        lower = jnp.where(row >= column, 1.0, 0.0)
        logs = jnp.log(retention[...]).T
        before = jnp.zeros((1, LANES), jnp.float32)
        place = lax.broadcasted_iota(jnp.int32, (HALO, LANES), 0)
        half = jnp.zeros((HALO, LANES), jnp.float32)
        for block in range(blocks):
            part = slice(block * BLOCK, (block + 1) * BLOCK)
            within = jnp.dot(lower, logs[part], precision=lax.Precision.HIGHEST)
            end = within[BLOCK - 1 : BLOCK]
            rise[part] = pairs(jnp.exp(0.5 * end - within))
            fall[part] = pairs(jnp.exp(within - 0.5 * end))
            reach[part] = pairs(jnp.exp(before + within))
            half = jnp.where(place == block, jnp.exp(0.5 * end), half)
            before = before + end
        decay[...] = jnp.broadcast_to(before, decay.shape)
        for offset in range(1, 4):
            @pl.when(seq + offset < 4)
            def _(offset=offset):
                sent_decay(offset).start()
        for chunk in range(chunks):
            at = slice(chunk * CHUNK, (chunk + 1) * CHUNK)
            picks[:, at] = selector(heads, head_width, chunk * CHUNK, CHUNK)
            halves[:, at] = jnp.dot(pairs(half), picks[:, at], preferred_element_type=jnp.float32)

        def norm_rows(i, _):
            part = span(i * 64, 64, 64)
            normed[span(HALO + i * 64, 64, 16)] = norm(tokens[part]).astype(jnp.bfloat16)
            return 0
        lax.fori_loop(0, rows // 64, norm_rows, 0)
        halo_copy.wait()
        kept = jnp.where(seq == 0, 0.0, 1.0)
        normed[:HALO] = (norm(halo[...]) * kept).astype(jnp.bfloat16)

    def weigh():
        for offset in range(1, 4):
            @pl.when(seq + offset < 4)
            def _(offset=offset):
                sent_decay(offset).wait_send()

            @pl.when(seq - offset >= 0)
            def _(offset=offset):
                got_decay(offset).wait_recv()
        place = lax.broadcasted_iota(jnp.int32, (HALO, LANES), 0)
        total = jnp.zeros((HALO, LANES), jnp.float32)
        for later in range(1, 4):
            log = jnp.where(later < seq, decays[later][:1], 0.0)
            total = total + jnp.where(place < later, log, 0.0)
        share_of = pairs(jnp.where(place < seq, jnp.exp(total), 0.0))
        for chunk in range(chunks):
            at = slice(chunk * CHUNK, (chunk + 1) * CHUNK)
            shares[:, at] = jnp.dot(share_of, picks[:, at], preferred_element_type=jnp.float32)

    def work(group, unit):
        at = pl.ds(unit * UNIT, UNIT)
        block = weights[group, :, :, at].reshape(features, UNIT)
        projected = jnp.dot(normed[...], block, preferred_element_type=jnp.float32)
        padded[...] = projected.astype(jnp.bfloat16).astype(jnp.float32)

    def convolve(group, unit):
        columns = span(group * GROUP + unit * UNIT, UNIT, UNIT)
        count = taps.shape[0]
        total = jnp.zeros((rows, UNIT), jnp.float32) + bias[:, columns]
        for k in range(count):
            start = HALO - (count - 1) + k
            total = total + taps[k : k + 1, columns] * padded[start : start + rows]
        active = (total / (1.0 + jnp.exp(-total))).astype(jnp.bfloat16)
        activated[:, columns] = active
        maps[...] += lax.dot_general(active, state_weight[:, columns], (((1,), (1,)), ((), ())),
                                     preferred_element_type=jnp.float32)
        factor = jnp.dot(rise[...], picks[:, columns], preferred_element_type=jnp.float32)
        scaled[:, columns] = (active.astype(jnp.float32) * factor).astype(jnp.bfloat16)

    def widen(chunk):
        at = pl.ds(chunk * CHUNK, CHUNK)
        reaches[:, at] = jnp.dot(reach[...], picks[:, at], preferred_element_type=jnp.float32)
        falls[:, at] = jnp.dot(fall[...], picks[:, at], preferred_element_type=jnp.float32)

    def within_groups(group):
        return jnp.logical_and(group >= 0, group < groups)

    order = ((0, 0, 0, "share"), (1, 0, 1, "arrive"), (0, 1, 1, "share"), (1, 1, 2, "share"))

    def parts(t, m, after):
        for part, unit, at, point in order:
            if at == m and point == after:
                @pl.when(within_groups(t - LAG_WORK))
                def _():
                    (work, convolve)[part](t - LAG_WORK, unit)

    def step(t, _):
        for m in range(3):
            ahead = FIRST if m == 0 else 0

            @pl.when(within_groups(t + ahead))
            def _():
                arrive(t + ahead, m)
            parts(t, m, "arrive")
            for lag, action in ((LAG_TURN, turn), (LAG_SHARE, share)):
                back, which = (lag + 2 - m) // 3, (m - lag) % 3
                back = back - FIRST if which == 0 else back

                @pl.when(within_groups(t - back))
                def _():
                    action(t - back, which)
                if lag == LAG_TURN:
                    parts(t, m, "turn")
            if m == 0:
                for start, needed, lead in leads:
                    on = within_groups(t + lead)
                    on = on if needed is None else jnp.logical_and(needed, on)

                    @pl.when(on)
                    def _():
                        start(t + lead)

                @pl.when(t == -FIRST)
                def _():
                    prepare()

                @pl.when(t == 2)
                def _():
                    weigh()

                @pl.when(within_groups(t - LAG_WORK))
                def _():
                    collect(t - LAG_WORK)
            for chunk in range(m, chunks, 3):
                @pl.when(t == 1 + chunk // 3)
                def _():
                    widen(chunk)
            parts(t, m, "share")
            @pl.when(within_groups(t - LAG_WORK))
            def _():
                settle(t - LAG_WORK, m)
        return 0

    lax.fori_loop(-FIRST, groups + LAG_WORK, step, 0)

    reads[...] = maps[:, entries:].astype(jnp.bfloat16)
    across[...] = jnp.zeros_like(across)
    for block in range(1, blocks):
        across[(block - 1) * BLOCK : block * BLOCK, (block - 1) * entries : block * entries] = (
            maps[block * BLOCK : (block + 1) * BLOCK, entries:].astype(jnp.bfloat16))
    row = lax.broadcasted_iota(jnp.int32, (BLOCK, BLOCK), 0)
    column = lax.broadcasted_iota(jnp.int32, (BLOCK, BLOCK), 1)
    turned = maps[...].T
    for block in range(blocks):
        part = slice(block * BLOCK, (block + 1) * BLOCK)
        writes = turned[:entries, part]
        scores = jnp.dot(maps[part, entries:], writes, precision=lax.Precision.HIGHEST)
        left[block, :BLOCK] = jnp.where(row >= column, scores, 0.0).astype(jnp.bfloat16)
        high, low = split_rows(writes)
        left[block, BLOCK : BLOCK + entries] = high
        left[block, BLOCK + entries :] = low

    def sent_state(chunk, offset):
        return remote(state.at[chunk], states.at[seq, chunk], state_send.at[chunk, offset],
                      state_recv.at[chunk, offset], (doc, seq + offset))

    def got_state(chunk, offset):
        return remote(state.at[chunk], states.at[seq - offset, chunk], state_send.at[chunk, offset],
                      state_recv.at[chunk, offset], sibling)

    def scan(chunk, _):
        at = span(chunk * CHUNK, CHUNK, CHUNK)
        half_of = halves[:, at]
        carried = jnp.zeros((entries, CHUNK), jnp.float32)
        inside, enter = [], []
        for block in range(blocks):
            part = slice(block * BLOCK, (block + 1) * BLOCK)
            both = jnp.dot(left[block], scaled[part, at], preferred_element_type=jnp.float32)
            half = half_of[block : block + 1]
            entering = half * carried
            inside.append(both[:BLOCK])
            enter.append(entering.astype(jnp.bfloat16))
            carried = half * (both[BLOCK : BLOCK + entries] + both[BLOCK + entries :] + entering)
        state[chunk] = carried.astype(jnp.bfloat16)
        crossed = jnp.dot(across[...], jnp.concatenate(enter[1:], axis=0), preferred_element_type=jnp.float32)
        for block in range(blocks):
            part = slice(block * BLOCK, (block + 1) * BLOCK)
            value = inside[block]
            if block > 0:
                value = value + crossed[(block - 1) * BLOCK : block * BLOCK]
            value = value * falls[part, at] + skip[:, at] * activated[part, at].astype(jnp.float32)
            local[chunk, part] = value
        for offset in range(1, 4):
            @pl.when(seq + offset < 4)
            def _(offset=offset):
                sent_state(chunk, offset).start()
        return 0

    lax.fori_loop(0, chunks, scan, 0)
    def out_copy(chunk):
        return pltpu.make_async_copy(emitted.at[chunk], result.at[chunk], out_sem.at[chunk])

    def finish(chunk, _):
        at = span(chunk * CHUNK, CHUNK, CHUNK)
        for offset in range(1, 4):
            @pl.when(seq - offset >= 0)
            def _(offset=offset):
                got_state(chunk, offset).wait_recv()
        incoming = jnp.zeros((entries, CHUNK), jnp.float32)
        for place in range(3):
            incoming = incoming + shares[place : place + 1, at] * states[place, chunk].astype(jnp.float32)
        more = jnp.dot(reads[...], incoming.astype(jnp.bfloat16), preferred_element_type=jnp.float32)
        emitted[chunk] = (local[chunk] + reaches[:, at] * more).astype(jnp.bfloat16)
        out_copy(chunk).start()
        return 0

    lax.fori_loop(0, chunks, finish, 0)
    for chunk in range(chunks):
        out_copy(chunk).wait()
        for offset in range(1, 4):
            @pl.when(seq + offset < 4)
            def _(chunk=chunk, offset=offset):
                sent_state(chunk, offset).wait_send()


def place_kernel(source, result, held, load_sem, out_sem):
    chunks, _, width = source.shape
    loads = [pltpu.make_async_copy(source.at[i], held.at[i], load_sem.at[i]) for i in range(chunks)]
    stores = [pltpu.make_async_copy(held.at[i], result.at[:, pl.ds(i * width, width)], out_sem.at[i])
              for i in range(chunks)]
    for copy in loads:
        copy.start()
    for load, store in zip(loads, stores):
        load.wait()
        store.start()
    for copy in stores:
        copy.wait()


def fused(tokens, norm_gain, in_weight, conv_weight, conv_bias, state_weight, skip_gain, retention):
    rows, features = tokens.shape[1:]
    depth, inner = in_weight.shape
    heads = retention.shape[2]
    docs = features // depth
    entries = state_weight.shape[1] // 2
    groups, chunks, blocks = inner // GROUP, inner // CHUNK, rows // BLOCK
    dma = pltpu.SemaphoreType.DMA
    vmem = pltpu.VMEM
    bf16, f32 = jnp.bfloat16, jnp.float32
    shape = jax.ShapeDtypeStruct
    emitted = pl.pallas_call(
        functools.partial(fused_kernel, inner // heads),
        out_shape=shape((chunks, rows, CHUNK), bf16),
        in_specs=[FAR] * 8,
        out_specs=FAR,
        scratch_shapes=[
            vmem((groups, docs, depth, GROUP), bf16), vmem((rows, features), bf16), vmem((HALO, features), bf16),
            vmem((HALO + rows, features), bf16), vmem((HALO + rows, UNIT), f32), vmem((rows, inner), bf16),
            vmem((rows, inner), bf16), vmem((chunks, rows, CHUNK), f32), vmem((1, features), f32),
            vmem(conv_weight.shape, f32), vmem((1, inner), f32), vmem((2 * entries, inner), bf16),
            vmem((2 * heads, rows), f32), vmem((1, inner), f32), vmem((2 * heads, inner), bf16),
            vmem((rows, LANES), bf16), vmem((rows, LANES), bf16), vmem((rows, LANES), bf16),
            vmem((HALO, inner), f32), vmem((HALO, inner), f32), vmem((rows, 2 * entries), f32),
            vmem((rows, entries), bf16), vmem((rows - BLOCK, (blocks - 1) * entries), bf16), vmem((rows, inner), f32),
            vmem((rows, inner), f32), vmem((blocks, BLOCK + 2 * entries, BLOCK), bf16),
            vmem((chunks, entries, CHUNK), bf16), vmem((4, chunks, entries, CHUNK), bf16),
            vmem((chunks, rows, CHUNK), bf16), vmem((8, LANES), f32), vmem((4, 8, LANES), f32),
            dma((8,)), dma((2,)), dma((groups, 4)), dma((groups, 4))] + [dma((groups, 3))] * 10 + [
            dma((groups, 4)), dma((groups,)), dma((2, 4)), dma((chunks, 4)), dma((chunks, 4)), dma((chunks,))],
        compiler_params=pltpu.CompilerParams(
            collective_id=2, has_side_effects=True, vmem_limit_bytes=60 * 1024 * 1024),
        name="fused",
    )(in_weight, tokens[0], norm_gain[None], conv_weight, conv_bias[None], state_weight.T, retention[0].T,
      skip_gain[None])
    result = pl.pallas_call(
        place_kernel,
        out_shape=shape((rows, inner), bf16),
        in_specs=[FAR],
        out_specs=FAR,
        scratch_shapes=[vmem(emitted.shape, bf16), dma((chunks,)), dma((chunks,))],
        compiler_params=pltpu.CompilerParams(vmem_limit_bytes=60 * 1024 * 1024),
        name="place",
    )(emitted)
    return result[None]


def body(tokens, norm_gain, in_weight, conv_weight, conv_bias, state_weight, skip_gain, retention):
    rows, features = tokens.shape[1:]
    inner = in_weight.shape[1]
    heads = retention.shape[2]
    head_width = inner // heads
    entries = state_weight.shape[1] // 2
    blocks = rows // BLOCK
    steps = inner // WIDTH
    taps = conv_weight.shape[0]
    count = lax.axis_size("seq")
    seq = lax.axis_index("seq")

    if (lax.axis_size("doc") == 8 and count == 4 and in_weight.shape[0] % 64 == 0 and heads == 64 and inner % CHUNK == 0
            and rows % BLOCK == 0):
        return fused(tokens, norm_gain, in_weight, conv_weight, conv_bias, state_weight, skip_gain, retention)

    full, halo = gather_weights(in_weight, tokens)

    log_rates = jnp.log(retention[0]).reshape(blocks, BLOCK, heads)
    lower = jnp.tril(jnp.ones((BLOCK, BLOCK), jnp.float32))
    within = jnp.einsum("ij,bjh->bih", lower, log_rates, precision=lax.Precision.HIGHEST)
    ends = within[:, -1]
    middle = 0.5 * ends
    rise = jnp.exp(middle[:, None] - within).reshape(rows, heads)
    fall = jnp.exp(within - middle[:, None]).reshape(rows, heads)
    half = jnp.exp(middle)

    def paired(value):
        high = lax.reduce_precision(value, 8, 7)
        return jnp.concatenate([high, value - high], axis=1).astype(jnp.bfloat16)

    rise, fall = paired(rise), paired(fall)
    half = jnp.pad(paired(half), ((0, -blocks % 16), (0, 0)))

    whole = lambda shape: pl.BlockSpec(shape, lambda j: (0,) * len(shape))
    params = pltpu.CompilerParams(vmem_limit_bytes=48 * 1024 * 1024)
    activated, maps, state = pl.pallas_call(
        functools.partial(project_kernel, head_width),
        grid=(steps,),
        out_shape=(jax.ShapeDtypeStruct((rows, inner), jnp.bfloat16),
                   jax.ShapeDtypeStruct((rows, 2 * entries), jnp.float32),
                   jax.ShapeDtypeStruct((entries, inner), jnp.bfloat16)),
        in_specs=[
            whole((rows, features)), whole((HALO, features)), whole((1, features)),
            pl.BlockSpec((full.shape[0], WIDTH), lambda j: (0, j)),
            pl.BlockSpec((taps, WIDTH), lambda j: (0, j)),
            pl.BlockSpec((1, WIDTH), lambda j: (0, j)),
            pl.BlockSpec((WIDTH, 2 * entries), lambda j: (j, 0)),
            whole(rise.shape), whole(half.shape),
        ],
        out_specs=(whole((rows, inner)), whole((rows, 2 * entries)), whole((entries, inner))),
        scratch_shapes=[pltpu.VMEM((HALO + rows, features), jnp.bfloat16),
                        pltpu.VMEM((HALO + rows, WIDTH), jnp.float32)],
        compiler_params=params,
        name="project",
    )(tokens[0], halo, norm_gain[None], full, conv_weight, conv_bias[None], state_weight, rise,
      half)

    decay = jnp.broadcast_to(jnp.pad(jnp.sum(ends, axis=0), (0, LANES - heads)), (8, LANES))
    states, decays = exchange_states(state, decay)
    index = jnp.arange(count)
    later = (index[None, :] > index[:, None]) & (index[None, :] < seq)
    logs = jnp.sum(jnp.where(later[:, :, None], decays[None, :, 0, :heads], 0.0), axis=1)
    shares = jnp.where(index[:, None] < seq, jnp.exp(logs), 0.0)
    shares = jnp.repeat(shares, head_width, axis=1)
    incoming = jnp.sum(shares[:, None] * states.astype(jnp.float32), axis=0)

    result = pl.pallas_call(
        functools.partial(scan_kernel, head_width),
        grid=(steps,),
        out_shape=jax.ShapeDtypeStruct((rows, inner), jnp.bfloat16),
        in_specs=[
            pl.BlockSpec((rows, WIDTH), lambda j: (0, j)),
            whole((rows, 2 * entries)),
            pl.BlockSpec((entries, WIDTH), lambda j: (0, j)),
            whole(rise.shape), whole(fall.shape), whole(half.shape),
            pl.BlockSpec((1, WIDTH), lambda j: (0, j)),
        ],
        out_specs=pl.BlockSpec((rows, WIDTH), lambda j: (0, j)),
        scratch_shapes=[pltpu.VMEM((blocks, BLOCK + 2 * entries, BLOCK), jnp.bfloat16)],
        compiler_params=params,
        name="scan",
    )(activated, maps, incoming, rise, fall, half, skip_gain[None])
    return result[None]


def solution(mesh):
    return jax.shard_map(
        body,
        mesh=mesh,
        in_specs=(
            P("doc", "seq", None),
            P(),
            P("doc", None),
            P(),
            P(),
            P(),
            P(),
            P("doc", "seq", None),
        ),
        out_specs=P("doc", "seq", None),
        check_vma=False,
    )
```
